512 devices in a mesh: dp: 128 (over z, y, core), rep: 4 (over x).
Axes of the slice: x: 4, y: 8, z: 8, core: 2. Of those that a mesh axis runs over, the one named last changes fastest.
Arguments:
- grads: bfloat16 [4, 128, 128, 4096], P('rep', 'dp')
- check_weights: int32 [4, 128, 8, 16], P('rep', 'dp'), may hold values from 1 to 8
Outputs:
- reduced: bfloat16 [128, 4096], P(None, 'dp')
- checksums: bfloat16 [8, 4096], P(None, 'dp')
The draws below stay inside these ranges and needn't reach their ends.
All inputs are finite; a program needn't handle non-finite values.
Results may differ from the reference program's by a relative error of at most 0.0039.
Values may be sent and summed in bfloat16 or wider, within the bound.
A program may use at most 64 MiB of HBM per device.

```python
import jax
import jax.numpy as jnp
from jax import lax

D = 4096
ROWS = 128
BLOCK = 16
BLOCKS = 8
DPS = 128
REPS = 4


def draw_grads(key, part):
    first, second = jax.random.split(jax.random.fold_in(key, 11), 2)
    shape = (REPS, DPS, ROWS, D)
    ramp = 1.0 + 2.0 * jnp.arange(D, dtype=jnp.float32) / (D - 1)
    spread = jax.random.uniform(second, (D,), jnp.float32, 0.7, 1.4)
    values = jax.random.normal(first, shape, jnp.float32) * (ramp * spread)
    return values.astype(jnp.bfloat16)


def place_ends(values, stream_key, smallest, top_value):
    shape = values.shape
    index_at = [jax.random.randint(jax.random.fold_in(stream_key, axis), (), 0, shape[axis]) for axis in range(len(shape))]
    values = values.at[tuple(index_at)].set(smallest)
    longest = shape.index(max(shape))
    index_at[longest] = (index_at[longest] + 1) % shape[longest]
    return values.at[tuple(index_at)].set(top_value)


def setup_inputs(seed: int = 0) -> dict:
    keys = jax.random.split(jax.random.key(seed), 3)
    return {
        "grads": draw_grads(jax.random.fold_in(keys[2], 71), 0),
        "check_weights": place_ends(jax.random.randint(keys[1], (REPS, DPS, BLOCKS, BLOCK), 1, 9), jax.random.fold_in(keys[1], 1), 1, 8).astype(jnp.int32),
    }


def reference(grads, check_weights):

    def add_group(carry, pair):
        block, weights = pair
        wsum = lax.optimization_barrier(jnp.sum(weights, axis=-1)).astype(jnp.float32)
        data = block.astype(jnp.float32)
        shaped = data.reshape(data.shape[0], BLOCKS, BLOCK, data.shape[-1])
        local = jnp.einsum('dkb,dkbe->dke', weights.astype(jnp.float32), shaped)
        local = local / wsum[:, :, None]
        return ((carry[0] + lax.optimization_barrier(jnp.sum(data, axis=0)), carry[1] + lax.optimization_barrier(jnp.sum(local, axis=0))), None)
    start = (jnp.zeros((ROWS, D), jnp.float32), jnp.zeros((BLOCKS, D), jnp.float32))
    (summed, check_sum), unused = lax.scan(add_group, start, (grads, check_weights))
    square = jnp.sum(summed * summed)
    factor = jnp.minimum(1.0, 2.0 * jnp.sqrt(jnp.float32(ROWS * D)) / jnp.sqrt(square + 1e-06))
    return ((factor * summed).astype(jnp.bfloat16), (factor * check_sum).astype(jnp.bfloat16))
```

```python
import functools

import jax
import jax.numpy as jnp
from jax import lax
from jax.experimental import pallas as pl
from jax.experimental.pallas import tpu as pltpu
from jax.sharding import Mesh
from jax.sharding import PartitionSpec as P

MESH = pl.DeviceIdType.MESH
BF, F32 = jnp.bfloat16, jnp.float32
LANES = 128


def far_first(n):
    return sorted(range(1, n), key=lambda o: -min(o, n - o))


def kernel(sizes, limit, g_ref, w_ref, out_ref, chk_ref, own, par, wpar, sa, sb, ra, rb, sa2, sb2, ra2, rb2,
           x3, grp, nsend, nrm, xt, chk, own_sem, w_sem, s0_send, s0_recv, s1_send, s1_recv, s2_send, s2_recv,
           x_sem, g_sem, n_sem):
    Z, Y, X = sizes
    YH = Y // 2
    z, y, c, x = (lax.axis_index(a) for a in ("z", "y", "c", "x"))
    yh, p = y // 2, lax.rem(y, 2)
    other = 1 - c

    def remote(src, dst, send, recv, **at):
        return pltpu.make_async_remote_copy(
            src_ref=src, dst_ref=dst, send_sem=send, recv_sem=recv, device_id=at, device_id_type=MESH
        )

    def drained(ref, sem):
        pltpu.make_async_copy(ref, ref, sem).wait()

    half = pl.ds(pl.multiple_of(c * 64, 64), 64)
    mine = pltpu.make_async_copy(g_ref.at[half], own, own_sem)
    mine.start()

    barrier = pltpu.get_barrier_semaphore()
    pl.semaphore_signal(barrier, inc=1, device_id={"c": other}, device_id_type=MESH)
    for o in far_first(Y):
        pl.semaphore_signal(barrier, inc=1, device_id={"y": lax.rem(y + o, Y)}, device_id_type=MESH)
    for o in far_first(Z):
        pl.semaphore_signal(barrier, inc=1, device_id={"z": lax.rem(z + o, Z)}, device_id_type=MESH)
    for o in far_first(X):
        pl.semaphore_signal(barrier, inc=1, device_id={"x": lax.rem(x + o, X)}, device_id_type=MESH)
    twin = 2 * yh + 1 - p
    pl.semaphore_signal(barrier, inc=1, device_id={"y": twin, "c": other}, device_id_type=MESH)
    pl.semaphore_wait(barrier, Y + Z + X - 3 + 2)

    remote(w_ref, wpar, w_sem.at[0], w_sem.at[1], c=other).start()
    for q in (0, 2, 3, 1):
        rows = pl.ds(pl.multiple_of(other * 64 + 16 * q, 16), 16)
        remote(g_ref.at[rows], par.at[q], s0_send, s0_recv.at[q], c=other).start()

    eye = lax.broadcasted_iota(jnp.int32, (16, 16), 0) == lax.broadcasted_iota(jnp.int32, (16, 16), 1)

    def columns(ref):
        w = ref[...].astype(F32)
        w = w / jnp.sum(w, axis=1, keepdims=True)
        row = lax.broadcasted_iota(jnp.int32, w.shape, 0)
        cols = []
        for q in range(4):
            one = jnp.sum(jnp.where(row == 4 * c + q, w, 0.0), axis=0, keepdims=True)
            col = jnp.sum(jnp.where(eye, jnp.broadcast_to(one, (16, 16)), 0.0), axis=1, keepdims=True)
            cols.append(jnp.broadcast_to(col, (16, LANES)))
        return cols

    mine.wait()
    drained(w_ref, w_sem.at[1])
    w_own, w_par = columns(w_ref), columns(wpar)

    for q in (0, 2, 3, 1):
        drained(par.at[q], s0_recv.at[q])
        pq = q % 2
        for t in range(Z * YH):
            zt, yt = t // YH, t % YH
            lanes = slice(t * LANES, (t + 1) * LANES)
            a = own[16 * q : 16 * q + 16, lanes].astype(F32)
            b = par[q, :, lanes].astype(F32)
            both = (a + b).astype(BF)
            check = jnp.sum(a * w_own[q] + b * w_par[q], axis=0, keepdims=True)
            high = check.astype(BF)
            low = (check - high.astype(F32)).astype(BF)
            to, at, i, n = (sa, 2 * yt + pq, zt, Z) if q < 2 else (sb, zt, 2 * yt + pq, Y)
            to[at, 16 * i : 16 * i + 16, :] = both
            to[at, 16 * n + i : 16 * n + i + 1, :] = high
            to[at, 16 * n + 8 + i : 16 * n + 9 + i, :] = low
        if q == 3:
            for o in far_first(Z):
                to = lax.rem(z + o, Z)
                remote(sb.at[to], rb.at[o - 1], s1_send.at[1], s1_recv.at[1], z=to).start()
        if q == 1:
            for o in far_first(Y):
                to = lax.rem(y + o, Y)
                remote(sa.at[to], ra.at[o - 1], s1_send.at[0], s1_recv.at[0], y=to).start()

    def fold(s, r, me, n, s2):
        def block(t):
            rows = slice(16 * t, 16 * t + 16)
            acc = s[me, rows, :].astype(F32)
            for o in range(r.shape[0]):
                acc += r[o, rows, :].astype(F32)
            return acc

        for t in range(n):
            s2[t, 0:16, :] = block(t)
        last = block(n)
        check = last[0:8] + last[8:16]
        for t in range(n):
            s2[t, 16:24, :] = jnp.broadcast_to(check[t : t + 1], (8, LANES))

    drained(rb, s1_recv.at[1])
    fold(sb, rb, z, Y, sb2)
    for o in far_first(Y):
        to = lax.rem(y + o, Y)
        remote(sb2.at[to], rb2.at[o - 1], s2_send.at[1], s2_recv.at[1], y=to).start()
    drained(ra, s1_recv.at[0])
    fold(sa, ra, y, Z, sa2)
    for o in far_first(Z):
        to = lax.rem(z + o, Z)
        remote(sa2.at[to], ra2.at[o - 1], s2_send.at[0], s2_recv.at[0], z=to).start()

    def total(s2, r2, me):
        acc = s2[me]
        for o in range(r2.shape[0]):
            acc += r2[o]
        return acc

    drained(rb2, s2_recv.at[1])
    low_rows = total(sb2, rb2, y)
    drained(ra2, s2_recv.at[0])
    top_rows = total(sa2, ra2, z)
    x3[x, 0:16, :] = top_rows[0:16]
    x3[x, 16:32, :] = low_rows[0:16]
    row = lax.broadcasted_iota(jnp.int32, (8, LANES), 0)
    x3[x, 32:40, :] = jnp.where(row < 4, top_rows[16:24], low_rows[16:24])
    for o in far_first(X):
        remote(x3.at[x], x3.at[x], x_sem.at[0], x_sem.at[1], x=lax.rem(x + o, X)).start()
    drained(x3.at[pl.ds(0, X - 1)], x_sem.at[1])
    m = 2 * p + c
    acc = x3[0]
    for i in range(1, X):
        acc += x3[i]
    grp[m] = acc
    for at in ({"y": twin}, {"c": other}, {"y": twin, "c": other}):
        remote(grp.at[m], grp.at[m], g_sem.at[0], g_sem.at[1], **at).start()
    drained(grp.at[pl.ds(0, 3)], g_sem.at[1])

    parts = []
    for i in range(8):
        core, q = i // 4, i % 4
        parts.append(grp[2 * (q % 2) + core, 16 * (q // 2) : 16 * (q // 2) + 16, :])
    whole = jnp.concatenate(parts, axis=0)
    nsend[...] = jnp.sum(whole * whole, axis=0, keepdims=True)
    j = 0
    order = sorted(
        ((a, b) for a in range(Z) for b in range(YH) if a or b),
        key=lambda o: -(min(o[0], Z - o[0]) + 2 * min(o[1], YH - o[1])),
    )
    for dz, dy in order:
        at = {"z": lax.rem(z + dz, Z), "y": lax.rem(y + 2 * dy, Y)}
        remote(nsend, nrm.at[j], n_sem.at[0], n_sem.at[1], **at).start()
        j += 1

    xt[...] = whole.T
    for k in range(8):
        core, q = k // 4, k % 4
        r = 32 + 4 * (q // 2)
        chk[k : k + 1, :] = grp[2 * (q % 2) + core, r : r + 1, :]
    turned = pltpu.roll(chk[...], lax.rem(LANES - 32 * m, LANES), 1)[:, 0:32]
    columns_out = xt[pl.ds(pl.multiple_of(32 * m, 32), 32), :]

    drained(nrm, n_sem.at[1])
    square = nsend[...]
    square += jnp.sum(nrm[...], axis=0)
    square = jnp.sum(square, axis=1, keepdims=True)
    factor = jnp.minimum(1.0, limit / jnp.sqrt(square + 1e-06))
    out_ref[...] = (columns_out * factor).astype(BF)
    chk_ref[...] = (turned * factor).astype(BF)

    drained(w_ref, w_sem.at[0])
    drained(par, s0_send)
    drained(ra, s1_send.at[0])
    drained(rb, s1_send.at[1])
    drained(ra2, s2_send.at[0])
    drained(rb2, s2_send.at[1])
    drained(x3.at[pl.ds(0, X - 1)], x_sem.at[0])
    drained(grp.at[pl.ds(0, 3)], g_sem.at[0])
    drained(nrm, n_sem.at[0])


def body(sizes, grads, check_weights):
    Z, Y, X = sizes
    local, weights = grads[0, 0], check_weights[0, 0]
    rows, width = local.shape
    limit = 2.0 * float((rows * Z * (Y // 2) * LANES) ** 0.5)
    dma = pltpu.SemaphoreType.DMA
    vmem = pltpu.VMEM
    out, chk = pl.pallas_call(
        functools.partial(kernel, sizes, limit),
        out_shape=(jax.ShapeDtypeStruct((32, rows), BF), jax.ShapeDtypeStruct((8, 32), BF)),
        in_specs=[pl.BlockSpec(memory_space=pl.ANY), pl.BlockSpec(memory_space=vmem)],
        out_specs=(pl.BlockSpec(memory_space=vmem), pl.BlockSpec(memory_space=vmem)),
        scratch_shapes=[
            vmem((64, width), BF),
            vmem((4, 16, width), BF),
            vmem((8, 16), jnp.int32),
            vmem((Y, 16 * Z + 16, LANES), BF),
            vmem((Z, 16 * Y + 16, LANES), BF),
            vmem((Y - 1, 16 * Z + 16, LANES), BF),
            vmem((Z - 1, 16 * Y + 16, LANES), BF),
            vmem((Z, 24, LANES), F32),
            vmem((Y, 24, LANES), F32),
            vmem((Z - 1, 24, LANES), F32),
            vmem((Y - 1, 24, LANES), F32),
            vmem((X, 40, LANES), F32),
            vmem((4, 40, LANES), F32),
            vmem((1, LANES), F32),
            vmem((Z * (Y // 2) - 1, 1, LANES), F32),
            vmem((LANES, LANES), F32),
            vmem((8, LANES), F32),
            dma,
            dma((2,)),
            dma,
            dma((4,)),
            dma((2,)),
            dma((2,)),
            dma((2,)),
            dma((2,)),
            dma((2,)),
            dma((2,)),
            dma((2,)),
        ],
        compiler_params=pltpu.CompilerParams(collective_id=0, has_side_effects=True),
    )(local, weights)
    return out.T, chk


def solution(mesh):
    Z, Y, X = 8, 8, mesh.shape["rep"]
    torus = Mesh(mesh.devices.reshape(Z, Y, 2, X), ("z", "y", "c", "x"))
    dp = ("z", "y", "c")
    return jax.shard_map(
        functools.partial(body, (Z, Y, X)),
        mesh=torus,
        in_specs=(P("x", dp, None, None), P("x", dp, None, None)),
        out_specs=(P(None, dp), P(None, dp)),
        check_vma=False,
    )
```

```python
import functools

import jax
import jax.numpy as jnp
from jax import lax
from jax.experimental import pallas as pl
from jax.experimental.pallas import tpu as pltpu
from jax.sharding import Mesh
from jax.sharding import PartitionSpec as P

MESH = pl.DeviceIdType.MESH
BF, F32 = jnp.bfloat16, jnp.float32
LANES = 128
HBM = pltpu.MemorySpace.HBM


def far_first(n):
    return sorted(range(1, n), key=lambda o: -min(o, n - o))


def near(n):
    return [o for o in far_first(n) if min(o, n - o) <= 2]


def kernel(sizes, limit, g_ref, w_ref, out_ref, chk_ref, own, par, wown, wpar, sa, sb, ra, rb, ca, cb, rca, rcb,
           sa2, sb2, ra2, rb2, ca2, cb2, rca2, rcb2, x3, xc, grp, gc, nsend, nrm, xt, chk, own_sem, w_sem, hop,
           s0_send, s0_recv, s1_send, s1_recv, c1_send, c1_recv, s2_send, s2_recv, c2_send, c2_recv,
           x_sem, g_sem, n_sem):
    Z, Y, X = sizes
    YH = Y // 2
    z, y, c, x = (lax.axis_index(a) for a in ("z", "y", "c", "x"))
    yh, p = y // 2, lax.rem(y, 2)
    other = 1 - c

    def remote(src, dst, send, recv, at):
        pltpu.make_async_remote_copy(
            src_ref=src, dst_ref=dst, send_sem=send, recv_sem=recv, device_id=at, device_id_type=MESH
        ).start()

    def signal(sem, at):
        pl.semaphore_signal(sem, inc=1, device_id=at, device_id_type=MESH)

    def drained(ref, sem):
        pltpu.make_async_copy(ref, ref, sem).wait()

    half = pl.ds(pl.multiple_of(c * 64, 64), 64)
    weights = pltpu.make_async_copy(w_ref, wown, w_sem.at[2])
    weights.start()
    mine = pltpu.make_async_copy(g_ref.at[half], own, own_sem)
    mine.start()

    barrier = pltpu.get_barrier_semaphore()
    for o in near(Y):
        signal(barrier, {"y": lax.rem(y + o, Y)})
    for o in near(Z):
        signal(barrier, {"z": lax.rem(z + o, Z)})
    for o in far_first(X):
        signal(barrier, {"x": lax.rem(x + o, X)})
    signal(barrier, {"c": other})
    pl.semaphore_wait(barrier, len(near(Y)) + len(near(Z)) + X)

    for o in near(Y):
        signal(hop.at[0], {"y": lax.rem(y + o, Y)})
    for o in near(Z):
        signal(hop.at[1], {"z": lax.rem(z + o, Z)})
    for q in (0, 2, 3, 1):
        rows = pl.ds(pl.multiple_of(other * 64 + 16 * q, 16), 16)
        remote(g_ref.at[rows], par.at[q], s0_send, s0_recv.at[q], {"c": other})
    weights.wait()
    remote(wown, wpar, w_sem.at[0], w_sem.at[1], {"c": other})

    eye = lax.broadcasted_iota(jnp.int32, (16, 16), 0) == lax.broadcasted_iota(jnp.int32, (16, 16), 1)

    def columns(ref):
        w = ref[...].astype(F32)
        w = w / jnp.sum(w, axis=1, keepdims=True)
        row = lax.broadcasted_iota(jnp.int32, w.shape, 0)
        cols = []
        for q in range(4):
            one = jnp.sum(jnp.where(row == 4 * c + q, w, 0.0), axis=0, keepdims=True)
            col = jnp.sum(jnp.where(eye, jnp.broadcast_to(one, (16, 16)), 0.0), axis=1, keepdims=True)
            cols.append(jnp.broadcast_to(col, (16, LANES)))
        return cols

    w_own = columns(wown)
    mine.wait()
    drained(wpar, w_sem.at[1])
    w_par = columns(wpar)

    for q in (0, 2, 3, 1):
        drained(par.at[q], s0_recv.at[q])
        for t in range(Z * YH):
            zt, yt = t // YH, t % YH
            lanes = slice(t * LANES, (t + 1) * LANES)
            a = own[16 * q : 16 * q + 16, lanes].astype(F32)
            b = par[q, :, lanes].astype(F32)
            check = jnp.sum(a * w_own[q] + b * w_par[q], axis=0, keepdims=True)
            to, cto, at, i = (sa, ca, 2 * yt + q, zt) if q < 2 else (sb, cb, zt, 2 * yt + q - 2)
            to[at, 16 * i : 16 * i + 16, :] = (a + b).astype(BF)
            cto[at, i : i + 1, :] = check.astype(BF)
        if q == 3:
            pl.semaphore_wait(hop.at[1], len(near(Z)))
            for o in far_first(Z):
                to = lax.rem(z + o, Z)
                remote(sb.at[to], rb.at[o - 1], s1_send.at[1], s1_recv.at[1], {"z": to})
                remote(cb.at[to], rcb.at[o - 1], c1_send.at[1], c1_recv.at[1], {"z": to})
        if q == 1:
            pl.semaphore_wait(hop.at[0], len(near(Y)))
            for o in far_first(Y):
                to = lax.rem(y + o, Y)
                remote(sa.at[to], ra.at[o - 1], s1_send.at[0], s1_recv.at[0], {"y": to})
                remote(ca.at[to], rca.at[o - 1], c1_send.at[0], c1_recv.at[0], {"y": to})

    def fold(s, r, cs, cr, me, n, s2, c2):
        for t in range(n):
            rows = slice(16 * t, 16 * t + 16)
            acc = s[me, rows, :].astype(F32)
            for o in range(r.shape[0]):
                acc += r[o, rows, :].astype(F32)
            s2[t] = acc
        check = cs[me].astype(F32)
        for o in range(r.shape[0]):
            check += cr[o].astype(F32)
        for t in range(n):
            c2[t] = check[t : t + 1]

    drained(rb, s1_recv.at[1])
    drained(rcb, c1_recv.at[1])
    fold(sb, rb, cb, rcb, z, Y, sb2, cb2)
    for o in far_first(Y):
        to = lax.rem(y + o, Y)
        remote(sb2.at[to], rb2.at[o - 1], s2_send.at[1], s2_recv.at[1], {"y": to})
        remote(cb2.at[to], rcb2.at[o - 1], c2_send.at[1], c2_recv.at[1], {"y": to})
    drained(ra, s1_recv.at[0])
    drained(rca, c1_recv.at[0])
    fold(sa, ra, ca, rca, y, Z, sa2, ca2)
    for o in far_first(Z):
        to = lax.rem(z + o, Z)
        remote(sa2.at[to], ra2.at[o - 1], s2_send.at[0], s2_recv.at[0], {"z": to})
        remote(ca2.at[to], rca2.at[o - 1], c2_send.at[0], c2_recv.at[0], {"z": to})

    def total(s2, r2, me):
        acc = s2[me]
        for o in range(r2.shape[0]):
            acc += r2[o]
        return acc

    drained(rb2, s2_recv.at[1])
    drained(rcb2, c2_recv.at[1])
    x3[x, 16:32, :] = total(sb2, rb2, y)
    xc[x, 1] = total(cb2, rcb2, y)
    drained(ra2, s2_recv.at[0])
    drained(rca2, c2_recv.at[0])
    x3[x, 0:16, :] = total(sa2, ra2, z)
    xc[x, 0] = total(ca2, rca2, z)
    for o in far_first(X):
        at = {"x": lax.rem(x + o, X)}
        remote(x3.at[x], x3.at[x], x_sem.at[0], x_sem.at[1], at)
        remote(xc.at[x], xc.at[x], x_sem.at[2], x_sem.at[3], at)
    drained(x3.at[pl.ds(0, X - 1)], x_sem.at[1])
    drained(xc.at[pl.ds(0, X - 1)], x_sem.at[3])
    m = 2 * p + c
    acc, check = x3[0], xc[0]
    for i in range(1, X):
        acc += x3[i]
        check += xc[i]

    nsend[...] = jnp.sum(acc * acc, axis=0, keepdims=True)
    grp[m] = acc
    gc[m] = check
    order = sorted(
        ((a, b, k) for a in range(Z) for b in range(Y) for k in range(2) if a or b or k),
        key=lambda o: -(min(o[0], Z - o[0]) + min(o[1], Y - o[1])),
    )
    for j, (dz, dy, dc) in enumerate(order):
        at = {"z": lax.rem(z + dz, Z), "y": lax.rem(y + dy, Y), "c": lax.rem(c + dc, 2)}
        remote(nsend, nrm.at[j], n_sem.at[0], n_sem.at[1], at)
    twin = 2 * yh + 1 - p
    for at in ({"y": twin, "c": other}, {"y": twin, "c": c}, {"y": y, "c": other}):
        remote(grp.at[m], grp.at[m], g_sem.at[0], g_sem.at[1], at)
        remote(gc.at[m], gc.at[m], g_sem.at[2], g_sem.at[3], at)
    drained(grp.at[pl.ds(0, 3)], g_sem.at[1])
    drained(gc.at[pl.ds(0, 3)], g_sem.at[3])
    parts = []
    for i in range(8):
        core, q = i // 4, i % 4
        parts.append(grp[2 * (q % 2) + core, 16 * (q // 2) : 16 * (q // 2) + 16, :])
        chk[i : i + 1, :] = gc[2 * (q % 2) + core, q // 2]
    xt[...] = jnp.concatenate(parts, axis=0).T
    turned = pltpu.roll(chk[...], lax.rem(LANES - 32 * m, LANES), 1)[:, 0:32]
    columns_out = xt[pl.ds(pl.multiple_of(32 * m, 32), 32), :]

    drained(nrm, n_sem.at[1])
    square = nsend[...] + jnp.sum(nrm[...], axis=0)
    square = jnp.sum(square, axis=1, keepdims=True)
    factor = jnp.minimum(1.0, limit / jnp.sqrt(square + 1e-06))
    out_ref[...] = (columns_out * factor).astype(BF)
    chk_ref[...] = (turned * factor).astype(BF)

    drained(wown, w_sem.at[0])
    drained(par, s0_send)
    for ref, sem in (
        (ra, s1_send.at[0]), (rb, s1_send.at[1]), (rca, c1_send.at[0]), (rcb, c1_send.at[1]),
        (ra2, s2_send.at[0]), (rb2, s2_send.at[1]), (rca2, c2_send.at[0]), (rcb2, c2_send.at[1]),
        (x3.at[pl.ds(0, X - 1)], x_sem.at[0]), (xc.at[pl.ds(0, X - 1)], x_sem.at[2]),
        (grp.at[pl.ds(0, 3)], g_sem.at[0]), (gc.at[pl.ds(0, 3)], g_sem.at[2]), (nrm, n_sem.at[0]),
    ):
        drained(ref, sem)


def body(sizes, grads, check_weights):
    Z, Y, X = sizes
    local, weights = grads[0, 0], check_weights[0, 0]
    rows, width = local.shape
    limit = 2.0 * float((rows * Z * (Y // 2) * LANES) ** 0.5)
    dma = pltpu.SemaphoreType.DMA
    vmem = pltpu.VMEM
    out, chk = pl.pallas_call(
        functools.partial(kernel, sizes, limit),
        out_shape=(jax.ShapeDtypeStruct((32, rows), BF), jax.ShapeDtypeStruct((8, 32), BF)),
        in_specs=[pl.BlockSpec(memory_space=HBM)] * 2,
        out_specs=(pl.BlockSpec(memory_space=vmem), pl.BlockSpec(memory_space=vmem)),
        scratch_shapes=[
            vmem((64, width), BF),
            vmem((4, 16, width), BF),
            vmem((8, 16), jnp.int32),
            vmem((8, 16), jnp.int32),
            *(vmem((n, 16 * k, LANES), BF) for n, k in ((Y, Z), (Z, Y), (Y - 1, Z), (Z - 1, Y))),
            *(vmem((n, 8, LANES), BF) for n in (Y, Z, Y - 1, Z - 1)),
            *(vmem((n, 16, LANES), F32) for n in (Z, Y, Z - 1, Y - 1)),
            *(vmem((n, 1, LANES), F32) for n in (Z, Y, Z - 1, Y - 1)),
            vmem((X, 32, LANES), F32),
            vmem((X, 2, 1, LANES), F32),
            vmem((4, 32, LANES), F32),
            vmem((4, 2, 1, LANES), F32),
            vmem((1, LANES), F32),
            vmem((Z * Y * 2 - 1, 1, LANES), F32),
            vmem((LANES, LANES), F32),
            vmem((8, LANES), F32),
            dma,
            dma((3,)),
            pltpu.SemaphoreType.REGULAR((2,)),
            dma,
            dma((4,)),
            *(dma((2,)) for _ in range(8)),
            dma((4,)),
            dma((4,)),
            dma((2,)),
        ],
        compiler_params=pltpu.CompilerParams(collective_id=0, has_side_effects=True, vmem_limit_bytes=8 << 20),
    )(pltpu.with_memory_space_constraint(local, HBM), pltpu.with_memory_space_constraint(weights, HBM))
    return out.T, chk


def solution(mesh):
    Z, Y, X = 8, 8, mesh.shape["rep"]
    torus = Mesh(mesh.devices.reshape(Z, Y, 2, X), ("z", "y", "c", "x"))
    dp = ("z", "y", "c")
    return jax.shard_map(
        functools.partial(body, (Z, Y, X)),
        mesh=torus,
        in_specs=(P("x", dp, None, None), P("x", dp, None, None)),
        out_specs=(P(None, dp), P(None, dp)),
        check_vma=False,
    )
```

```python
import functools

import jax
import jax.numpy as jnp
from jax import lax
from jax.experimental import pallas as pl
from jax.experimental.pallas import tpu as pltpu
from jax.sharding import Mesh
from jax.sharding import PartitionSpec as P

MESH = pl.DeviceIdType.MESH
BF, F32 = jnp.bfloat16, jnp.float32
LANES = 128
HBM = pltpu.MemorySpace.HBM


def far_first(n):
    return sorted(range(1, n), key=lambda o: -min(o, n - o))


def near(n):
    return [o for o in far_first(n) if min(o, n - o) <= 2]


def kernel(sizes, limit, g_ref, w_ref, out_ref, chk_ref, own, par, wown, wpar, sa, sb, ra, rb, ca, cb, rca, rcb,
           sa2, sb2, ra2, rb2, ca2, cb2, rca2, rcb2, grp, gc, nsend, nrm, xt, chk, own_sem, w_sem, hop,
           s0_send, s0_recv, s1_send, s1_recv, c1_send, c1_recv, s2_send, s2_recv, c2_send, c2_recv,
           g_sem, n_sem):
    Z, Y, X = sizes
    YH = Y // 2
    z, y, c, x = (lax.axis_index(a) for a in ("z", "y", "c", "x"))
    yh, p = y // 2, lax.rem(y, 2)
    other = 1 - c

    def remote(src, dst, send, recv, at):
        pltpu.make_async_remote_copy(
            src_ref=src, dst_ref=dst, send_sem=send, recv_sem=recv, device_id=at, device_id_type=MESH
        ).start()

    def signal(sem, at):
        pl.semaphore_signal(sem, inc=1, device_id=at, device_id_type=MESH)

    def drained(ref, sem):
        pltpu.make_async_copy(ref, ref, sem).wait()

    half = pl.ds(pl.multiple_of(c * 64, 64), 64)
    weights = pltpu.make_async_copy(w_ref, wown, w_sem.at[2])
    weights.start()
    mine = pltpu.make_async_copy(g_ref.at[half], own, own_sem)
    mine.start()

    barrier = pltpu.get_barrier_semaphore()
    for o in near(Y):
        signal(barrier, {"y": lax.rem(y + o, Y)})
    for o in near(Z):
        signal(barrier, {"z": lax.rem(z + o, Z)})
    for o in far_first(X):
        signal(barrier, {"x": lax.rem(x + o, X)})
    signal(barrier, {"c": other})
    pl.semaphore_wait(barrier, len(near(Y)) + len(near(Z)) + X)

    for o in near(Y):
        signal(hop.at[0], {"y": lax.rem(y + o, Y)})
    for o in near(Z):
        signal(hop.at[1], {"z": lax.rem(z + o, Z)})
    for q in (0, 2, 3, 1):
        rows = pl.ds(pl.multiple_of(other * 64 + 16 * q, 16), 16)
        remote(g_ref.at[rows], par.at[q], s0_send, s0_recv.at[q], {"c": other})
    remote(w_ref, wpar, w_sem.at[0], w_sem.at[1], {"c": other})

    eye = lax.broadcasted_iota(jnp.int32, (16, 16), 0) == lax.broadcasted_iota(jnp.int32, (16, 16), 1)

    def columns(ref):
        w = ref[...].astype(F32)
        w = w / jnp.sum(w, axis=1, keepdims=True)
        row = lax.broadcasted_iota(jnp.int32, w.shape, 0)
        cols = []
        for q in range(4):
            one = jnp.sum(jnp.where(row == 4 * c + q, w, 0.0), axis=0, keepdims=True)
            col = jnp.sum(jnp.where(eye, jnp.broadcast_to(one, (16, 16)), 0.0), axis=1, keepdims=True)
            cols.append(jnp.broadcast_to(col, (16, LANES)))
        return cols

    weights.wait()
    w_own = columns(wown)
    mine.wait()
    drained(wpar, w_sem.at[1])
    w_par = columns(wpar)

    for q in (0, 2, 3, 1):
        drained(par.at[q], s0_recv.at[q])
        for t in range(Z * YH):
            zt, yt = t // YH, t % YH
            lanes = slice(t * LANES, (t + 1) * LANES)
            a = own[16 * q : 16 * q + 16, lanes].astype(F32)
            b = par[q, :, lanes].astype(F32)
            check = jnp.sum(a * w_own[q] + b * w_par[q], axis=0, keepdims=True)
            to, cto, at, i = (sa, ca, 2 * yt + q, zt) if q < 2 else (sb, cb, zt, 2 * yt + q - 2)
            to[at, 16 * i : 16 * i + 16, :] = (a + b).astype(BF)
            cto[at, i : i + 1, :] = check.astype(BF)
        if q == 3:
            pl.semaphore_wait(hop.at[1], len(near(Z)))
            for o in far_first(Z):
                to = lax.rem(z + o, Z)
                remote(sb.at[to], rb.at[o - 1], s1_send.at[1], s1_recv.at[1], {"z": to})
                remote(cb.at[to], rcb.at[o - 1], c1_send.at[1], c1_recv.at[1], {"z": to})
        if q == 1:
            pl.semaphore_wait(hop.at[0], len(near(Y)))
            for o in far_first(Y):
                to = lax.rem(y + o, Y)
                remote(sa.at[to], ra.at[o - 1], s1_send.at[0], s1_recv.at[0], {"y": to})
                remote(ca.at[to], rca.at[o - 1], c1_send.at[0], c1_recv.at[0], {"y": to})

    def fold(k, axis, held, me, n, s, r, cs, cr, s2, r2, c2, cr2):
        drained(cr, c1_recv.at[k])
        check = cs[held].astype(F32)
        for o in range(cr.shape[0]):
            check += cr[o].astype(F32)
        for t in range(n):
            c2[t] = check[t : t + 1]
        if k:
            drained(r, s1_recv.at[k])
        slot = x * n + me

        def block(o):
            to = lax.rem(me + o, n)
            rows = pl.ds(pl.multiple_of(16 * to, 16), 16)
            acc = s[held, rows, :].astype(F32)
            for i in range(r.shape[0]):
                acc += r[i, rows, :].astype(F32)
            s2[to] = acc.astype(BF)

        def send(o):
            to = lax.rem(me + o, n)
            for i in [*far_first(X), 0]:
                if o or i:
                    at = {axis: to, "x": lax.rem(x + i, X)}
                    remote(s2.at[to], r2.at[slot], s2_send.at[k], s2_recv.at[k], at)
                    remote(c2.at[to], cr2.at[slot], c2_send.at[k], c2_recv.at[k], at)

        order = [*far_first(n), 0]
        if k:
            for o in order:
                block(o)
            drained(ra, s1_recv.at[0])
            for o in order:
                send(o)
        else:
            for o in order:
                block(o)
                send(o)
        r2[slot] = s2[me]
        cr2[slot] = c2[me]

    fold(1, "y", z, y, Y, sb, rb, cb, rcb, sb2, rb2, cb2, rcb2)
    fold(0, "z", y, z, Z, sa, ra, ca, rca, sa2, ra2, ca2, rca2)

    def total(k, r2, cr2):
        drained(r2.at[pl.ds(0, r2.shape[0] - 1)], s2_recv.at[k])
        drained(cr2.at[pl.ds(0, r2.shape[0] - 1)], c2_recv.at[k])
        acc, check = r2[0].astype(F32), cr2[0]
        for i in range(1, r2.shape[0]):
            acc += r2[i].astype(F32)
            check += cr2[i]
        return acc, check

    low, low_check = total(1, rb2, rcb2)
    top, top_check = total(0, ra2, rca2)
    m = 2 * p + c

    nsend[...] = jnp.sum(top * top + low * low, axis=0, keepdims=True)
    grp[m, 0:16, :] = top
    grp[m, 16:32, :] = low
    gc[m, 0] = top_check
    gc[m, 1] = low_check
    order = sorted(
        ((a, b, k) for a in range(Z) for b in range(Y) for k in range(2) if a or b or k),
        key=lambda o: -(min(o[0], Z - o[0]) + min(o[1], Y - o[1])),
    )
    for j, (dz, dy, dc) in enumerate(order):
        at = {"z": lax.rem(z + dz, Z), "y": lax.rem(y + dy, Y), "c": lax.rem(c + dc, 2)}
        remote(nsend, nrm.at[j], n_sem.at[0], n_sem.at[1], at)
    twin = 2 * yh + 1 - p
    for at in ({"y": twin, "c": other}, {"y": twin, "c": c}, {"y": y, "c": other}):
        remote(grp.at[m], grp.at[m], g_sem.at[0], g_sem.at[1], at)
        remote(gc.at[m], gc.at[m], g_sem.at[2], g_sem.at[3], at)
    drained(grp.at[pl.ds(0, 3)], g_sem.at[1])
    drained(gc.at[pl.ds(0, 3)], g_sem.at[3])
    parts = []
    for i in range(8):
        core, q = i // 4, i % 4
        parts.append(grp[2 * (q % 2) + core, 16 * (q // 2) : 16 * (q // 2) + 16, :])
        chk[i : i + 1, :] = gc[2 * (q % 2) + core, q // 2]
    xt[...] = jnp.concatenate(parts, axis=0).T
    turned = pltpu.roll(chk[...], lax.rem(LANES - 32 * m, LANES), 1)[:, 0:32]
    columns_out = xt[pl.ds(pl.multiple_of(32 * m, 32), 32), :]

    drained(nrm, n_sem.at[1])
    square = nsend[...] + jnp.sum(nrm[...], axis=0)
    square = jnp.sum(square, axis=1, keepdims=True)
    factor = jnp.minimum(1.0, limit / jnp.sqrt(square + 1e-06))
    out_ref[...] = (columns_out * factor).astype(BF)
    chk_ref[...] = (turned * factor).astype(BF)

    drained(wown, w_sem.at[0])
    drained(par, s0_send)
    for ref, sem in (
        (ra, s1_send.at[0]), (rb, s1_send.at[1]), (rca, c1_send.at[0]), (rcb, c1_send.at[1]),
        (ra2.at[pl.ds(0, X * Z - 1)], s2_send.at[0]), (rb2.at[pl.ds(0, X * Y - 1)], s2_send.at[1]),
        (rca2.at[pl.ds(0, X * Z - 1)], c2_send.at[0]), (rcb2.at[pl.ds(0, X * Y - 1)], c2_send.at[1]),
        (grp.at[pl.ds(0, 3)], g_sem.at[0]), (gc.at[pl.ds(0, 3)], g_sem.at[2]), (nrm, n_sem.at[0]),
    ):
        drained(ref, sem)


def leave(out_ref, chk_ref, to_ref, chk_to_ref, sem):
    copies = [
        pltpu.make_async_copy(out_ref, to_ref, sem.at[0]),
        pltpu.make_async_copy(chk_ref, chk_to_ref, sem.at[1]),
    ]
    for copy in copies:
        copy.start()
    for copy in copies:
        copy.wait()


def body(sizes, grads, check_weights):
    Z, Y, X = sizes
    local, weights = grads[0, 0], check_weights[0, 0]
    rows, width = local.shape
    limit = 2.0 * float((rows * Z * (Y // 2) * LANES) ** 0.5)
    dma = pltpu.SemaphoreType.DMA
    vmem = pltpu.VMEM
    out, chk = pl.pallas_call(
        functools.partial(kernel, sizes, limit),
        out_shape=(jax.ShapeDtypeStruct((32, rows), BF), jax.ShapeDtypeStruct((8, 32), BF)),
        in_specs=[pl.BlockSpec(memory_space=HBM)] * 2,
        out_specs=(pl.BlockSpec(memory_space=vmem), pl.BlockSpec(memory_space=vmem)),
        scratch_shapes=[
            vmem((64, width), BF),
            vmem((4, 16, width), BF),
            vmem((8, 16), jnp.int32),
            vmem((8, 16), jnp.int32),
            *(vmem((n, 16 * k, LANES), BF) for n, k in ((Y, Z), (Z, Y), (Y - 1, Z), (Z - 1, Y))),
            *(vmem((n, 8, LANES), BF) for n in (Y, Z, Y - 1, Z - 1)),
            *(vmem((n, 16, LANES), BF) for n in (Z, Y, X * Z, X * Y)),
            *(vmem((n, 1, LANES), F32) for n in (Z, Y, X * Z, X * Y)),
            vmem((4, 32, LANES), F32),
            vmem((4, 2, 1, LANES), F32),
            vmem((1, LANES), F32),
            vmem((Z * Y * 2 - 1, 1, LANES), F32),
            vmem((LANES, LANES), F32),
            vmem((8, LANES), F32),
            dma,
            dma((3,)),
            pltpu.SemaphoreType.REGULAR((2,)),
            dma,
            dma((4,)),
            *(dma((2,)) for _ in range(8)),
            dma((4,)),
            dma((2,)),
        ],
        compiler_params=pltpu.CompilerParams(collective_id=0, has_side_effects=True, vmem_limit_bytes=8 << 20),
    )(pltpu.with_memory_space_constraint(local, HBM), pltpu.with_memory_space_constraint(weights, HBM))
    out, chk = pl.pallas_call(
        leave,
        out_shape=(jax.ShapeDtypeStruct((32, rows), BF), jax.ShapeDtypeStruct((8, 32), BF)),
        in_specs=[pl.BlockSpec(memory_space=pl.ANY)] * 2,
        out_specs=(pl.BlockSpec(memory_space=HBM), pl.BlockSpec(memory_space=HBM)),
        scratch_shapes=[dma((2,))],
        compiler_params=pltpu.CompilerParams(vmem_limit_bytes=1 << 20),
    )(out, chk)
    return out.T, chk


def solution(mesh):
    Z, Y, X = 8, 8, mesh.shape["rep"]
    torus = Mesh(mesh.devices.reshape(Z, Y, 2, X), ("z", "y", "c", "x"))
    dp = ("z", "y", "c")
    return jax.shard_map(
        functools.partial(body, (Z, Y, X)),
        mesh=torus,
        in_specs=(P("x", dp, None, None), P("x", dp, None, None)),
        out_specs=(P(None, dp), P(None, dp)),
        check_vma=False,
    )
```

```python
import functools

import jax
import jax.numpy as jnp
from jax import lax
from jax.experimental import pallas as pl
from jax.experimental.pallas import tpu as pltpu
from jax.sharding import Mesh
from jax.sharding import PartitionSpec as P

MESH = pl.DeviceIdType.MESH
BF, F32 = jnp.bfloat16, jnp.float32
LANES = 128
HBM = pltpu.MemorySpace.HBM


def far_first(n):
    return sorted(range(1, n), key=lambda o: -min(o, n - o))


def near(n):
    return [o for o in far_first(n) if min(o, n - o) <= 2]


def kernel(sizes, limit, g_ref, w_ref, out_ref, chk_ref, own, away, par, wown, wpar, sa, sb, ra, rb, ca, cb, rca, rcb,
           sa2, sb2, ra2, rb2, ca2, cb2, rca2, rcb2, grp, gc, nsend, nrm, xt, chk, own_sem, away_sem, w_sem, hop,
           s0_send, s0_recv, s1_send, s1_recv, c1_send, c1_recv, s2_send, s2_recv, c2_send, c2_recv,
           g_sem, n_sem):
    Z, Y, X = sizes
    YH = Y // 2
    z, y, c, x = (lax.axis_index(a) for a in ("z", "y", "c", "x"))
    yh, p = y // 2, lax.rem(y, 2)
    other = 1 - c

    def remote(src, dst, send, recv, at):
        pltpu.make_async_remote_copy(
            src_ref=src, dst_ref=dst, send_sem=send, recv_sem=recv, device_id=at, device_id_type=MESH
        ).start()

    def signal(sem, at):
        pl.semaphore_signal(sem, inc=1, device_id=at, device_id_type=MESH)

    def drained(ref, sem):
        pltpu.make_async_copy(ref, ref, sem).wait()

    half = pl.ds(pl.multiple_of(c * 64, 64), 64)
    weights = pltpu.make_async_copy(w_ref, wown, w_sem.at[2])
    weights.start()
    mine = pltpu.make_async_copy(g_ref.at[half], own, own_sem)
    mine.start()
    rest = pl.ds(pl.multiple_of(other * 64, 64), 64)
    theirs = pltpu.make_async_copy(g_ref.at[rest], away, away_sem)
    theirs.start()

    barrier = pltpu.get_barrier_semaphore()
    for o in near(Y):
        signal(barrier, {"y": lax.rem(y + o, Y)})
    for o in near(Z):
        signal(barrier, {"z": lax.rem(z + o, Z)})
    for o in far_first(X):
        signal(barrier, {"x": lax.rem(x + o, X)})
    signal(barrier, {"c": other})
    pl.semaphore_wait(barrier, len(near(Y)) + len(near(Z)) + X)

    for o in near(Y):
        signal(hop.at[0], {"y": lax.rem(y + o, Y)})
    for o in near(Z):
        signal(hop.at[1], {"z": lax.rem(z + o, Z)})
    theirs.wait()
    for q in (2, 3, 0, 1):
        remote(away.at[pl.ds(16 * q, 16)], par.at[q], s0_send, s0_recv.at[q], {"c": other})
    remote(w_ref, wpar, w_sem.at[0], w_sem.at[1], {"c": other})

    eye = lax.broadcasted_iota(jnp.int32, (16, 16), 0) == lax.broadcasted_iota(jnp.int32, (16, 16), 1)

    def columns(ref):
        w = ref[...].astype(F32)
        w = w / jnp.sum(w, axis=1, keepdims=True)
        row = lax.broadcasted_iota(jnp.int32, w.shape, 0)
        cols = []
        for q in range(4):
            one = jnp.sum(jnp.where(row == 4 * c + q, w, 0.0), axis=0, keepdims=True)
            col = jnp.sum(jnp.where(eye, jnp.broadcast_to(one, (16, 16)), 0.0), axis=1, keepdims=True)
            cols.append(jnp.broadcast_to(col, (16, LANES)))
        return cols

    weights.wait()
    w_own = columns(wown)
    mine.wait()
    drained(wpar, w_sem.at[1])
    w_par = columns(wpar)

    def place(t, me, n):
        return lax.rem(t - me - 2 + 2 * n, n)

    def spread(k, axis, me, n, s, r, h):
        half_rows = pl.ds(s.shape[1] // 2 * h, s.shape[1] // 2)
        for o in far_first(n):
            to = lax.rem(me + o, n)
            remote(s.at[to, half_rows], r.at[o - 1, half_rows], s1_send.at[k, h], s1_recv.at[k, h], {axis: to})

    def spread_checks(k, axis, me, n, cs, cr):
        for o in far_first(n):
            to = lax.rem(me + o, n)
            remote(cs.at[to], cr.at[o - 1], c1_send.at[k], c1_recv.at[k], {axis: to})

    for q in (2, 3, 0, 1):
        drained(par.at[q], s0_recv.at[q])
        for t in range(Z * YH):
            zt, yt = t // YH, t % YH
            lanes = slice(t * LANES, (t + 1) * LANES)
            a = own[16 * q : 16 * q + 16, lanes].astype(F32)
            b = par[q, :, lanes].astype(F32)
            check = jnp.sum(a * w_own[q] + b * w_par[q], axis=0, keepdims=True)
            if q < 2:
                to, cto, at, tile, i = sa, ca, 2 * yt + q, zt, place(zt, z, Z)
            else:
                to, cto, at, tile, i = sb, cb, zt, 2 * yt + q - 2, place(2 * yt + q - 2, y, Y)
            to[at, pl.ds(pl.multiple_of(16 * i, 16), 16), :] = (a + b).astype(BF)
            cto[at, tile : tile + 1, :] = check.astype(BF)
        if q == 3:
            pl.semaphore_wait(hop.at[1], len(near(Z)))
            spread_checks(1, "z", z, Z, cb, rcb)
            spread(1, "z", z, Z, sb, rb, 0)
    pl.semaphore_wait(hop.at[0], len(near(Y)))
    spread_checks(0, "y", y, Y, ca, rca)
    spread(0, "y", y, Y, sa, ra, 0)
    spread(1, "z", z, Z, sb, rb, 1)
    spread(0, "y", y, Y, sa, ra, 1)

    def fold_checks(k, held, cs, cr, c2):
        drained(cr, c1_recv.at[k])
        check = cs[held].astype(F32)
        for o in range(cr.shape[0]):
            check += cr[o].astype(F32)
        for t in range(c2.shape[0]):
            c2[t] = check[t : t + 1]

    def arrived(k, r, h):
        drained(r.at[:, pl.ds(r.shape[1] // 2 * h, r.shape[1] // 2)], s1_recv.at[k, h])

    def offsets(n, h):
        places = range(n // 2 * h, n // 2 * (h + 1))
        return sorted(((i + 2) % n for i in places), key=lambda o: -min(o, n - o))

    def block(h, held, me, n, s, r, s2):
        for o in offsets(n, h):
            i = (o - 2) % n
            rows = slice(16 * i, 16 * i + 16)
            acc = s[held, rows, :].astype(F32)
            for j in range(r.shape[0]):
                acc += r[j, rows, :].astype(F32)
            s2[lax.rem(me + o, n)] = acc.astype(BF)

    def give(k, h, axis, me, n, s2, r2, c2, cr2):
        slot = x * n + me
        for o in offsets(n, h):
            to = lax.rem(me + o, n)
            for i in [*far_first(X), 0]:
                if o or i:
                    at = {axis: to, "x": lax.rem(x + i, X)}
                    remote(s2.at[to], r2.at[slot], s2_send.at[k], s2_recv.at[k], at)
                    remote(c2.at[to], cr2.at[slot], c2_send.at[k], c2_recv.at[k], at)

    fold_checks(1, z, cb, rcb, cb2)
    arrived(1, rb, 0)
    block(0, z, y, Y, sb, rb, sb2)
    fold_checks(0, y, ca, rca, ca2)
    arrived(0, ra, 0)
    give(1, 0, "y", y, Y, sb2, rb2, cb2, rcb2)
    block(0, y, z, Z, sa, ra, sa2)
    give(0, 0, "z", z, Z, sa2, ra2, ca2, rca2)
    arrived(1, rb, 1)
    block(1, z, y, Y, sb, rb, sb2)
    give(1, 1, "y", y, Y, sb2, rb2, cb2, rcb2)
    arrived(0, ra, 1)
    block(1, y, z, Z, sa, ra, sa2)
    give(0, 1, "z", z, Z, sa2, ra2, ca2, rca2)
    rb2[x * Y + y], rcb2[x * Y + y] = sb2[y], cb2[y]
    ra2[x * Z + z], rca2[x * Z + z] = sa2[z], ca2[z]

    def total(k, r2, cr2):
        drained(r2.at[pl.ds(0, r2.shape[0] - 1)], s2_recv.at[k])
        drained(cr2.at[pl.ds(0, r2.shape[0] - 1)], c2_recv.at[k])
        acc, check = r2[0].astype(F32), cr2[0]
        for i in range(1, r2.shape[0]):
            acc += r2[i].astype(F32)
            check += cr2[i]
        return acc, check

    low, low_check = total(1, rb2, rcb2)
    top, top_check = total(0, ra2, rca2)
    m = 2 * p + c

    nsend[...] = jnp.sum(top * top + low * low, axis=0, keepdims=True)
    grp[m, 0:16, :] = top
    grp[m, 16:32, :] = low
    gc[m, 0] = top_check
    gc[m, 1] = low_check
    order = sorted(
        ((a, b, k) for a in range(Z) for b in range(Y) for k in range(2) if a or b or k),
        key=lambda o: -(min(o[0], Z - o[0]) + min(o[1], Y - o[1])),
    )
    for j, (dz, dy, dc) in enumerate(order):
        at = {"z": lax.rem(z + dz, Z), "y": lax.rem(y + dy, Y), "c": lax.rem(c + dc, 2)}
        remote(nsend, nrm.at[j], n_sem.at[0], n_sem.at[1], at)
    twin = 2 * yh + 1 - p
    for at in ({"y": twin, "c": other}, {"y": twin, "c": c}, {"y": y, "c": other}):
        remote(grp.at[m], grp.at[m], g_sem.at[0], g_sem.at[1], at)
        remote(gc.at[m], gc.at[m], g_sem.at[2], g_sem.at[3], at)
    drained(grp.at[pl.ds(0, 3)], g_sem.at[1])
    drained(gc.at[pl.ds(0, 3)], g_sem.at[3])
    parts = []
    for i in range(8):
        core, q = i // 4, i % 4
        parts.append(grp[2 * (q % 2) + core, 16 * (q // 2) : 16 * (q // 2) + 16, :])
        chk[i : i + 1, :] = gc[2 * (q % 2) + core, q // 2]
    xt[...] = jnp.concatenate(parts, axis=0).T
    turned = pltpu.roll(chk[...], lax.rem(LANES - 32 * m, LANES), 1)[:, 0:32]
    columns_out = xt[pl.ds(pl.multiple_of(32 * m, 32), 32), :]

    drained(nrm, n_sem.at[1])
    square = nsend[...] + jnp.sum(nrm[...], axis=0)
    square = jnp.sum(square, axis=1, keepdims=True)
    factor = jnp.minimum(1.0, limit / jnp.sqrt(square + 1e-06))
    out_ref[...] = (columns_out * factor).astype(BF)
    chk_ref[...] = (turned * factor).astype(BF)

    drained(wown, w_sem.at[0])
    drained(par, s0_send)
    for ref, sem in (
        *((r.at[:, pl.ds(r.shape[1] // 2 * h, r.shape[1] // 2)], s1_send.at[k, h]) for k, r in ((0, ra), (1, rb)) for h in (0, 1)),
        (rca, c1_send.at[0]), (rcb, c1_send.at[1]),
        (ra2.at[pl.ds(0, X * Z - 1)], s2_send.at[0]), (rb2.at[pl.ds(0, X * Y - 1)], s2_send.at[1]),
        (rca2.at[pl.ds(0, X * Z - 1)], c2_send.at[0]), (rcb2.at[pl.ds(0, X * Y - 1)], c2_send.at[1]),
        (grp.at[pl.ds(0, 3)], g_sem.at[0]), (gc.at[pl.ds(0, 3)], g_sem.at[2]), (nrm, n_sem.at[0]),
    ):
        drained(ref, sem)


def leave(out_ref, chk_ref, to_ref, chk_to_ref, sem):
    copies = [
        pltpu.make_async_copy(out_ref, to_ref, sem.at[0]),
        pltpu.make_async_copy(chk_ref, chk_to_ref, sem.at[1]),
    ]
    for copy in copies:
        copy.start()
    for copy in copies:
        copy.wait()


def body(sizes, grads, check_weights):
    Z, Y, X = sizes
    local, weights = grads[0, 0], check_weights[0, 0]
    rows, width = local.shape
    limit = 2.0 * float((rows * Z * (Y // 2) * LANES) ** 0.5)
    dma = pltpu.SemaphoreType.DMA
    vmem = pltpu.VMEM
    out, chk = pl.pallas_call(
        functools.partial(kernel, sizes, limit),
        out_shape=(jax.ShapeDtypeStruct((32, rows), BF), jax.ShapeDtypeStruct((8, 32), BF)),
        in_specs=[pl.BlockSpec(memory_space=HBM)] * 2,
        out_specs=(pl.BlockSpec(memory_space=vmem), pl.BlockSpec(memory_space=vmem)),
        scratch_shapes=[
            vmem((64, width), BF),
            vmem((64, width), BF),
            vmem((4, 16, width), BF),
            vmem((8, 16), jnp.int32),
            vmem((8, 16), jnp.int32),
            *(vmem((n, 16 * k, LANES), BF) for n, k in ((Y, Z), (Z, Y), (Y - 1, Z), (Z - 1, Y))),
            *(vmem((n, 8, LANES), BF) for n in (Y, Z, Y - 1, Z - 1)),
            *(vmem((n, 16, LANES), BF) for n in (Z, Y, X * Z, X * Y)),
            *(vmem((n, 1, LANES), F32) for n in (Z, Y, X * Z, X * Y)),
            vmem((4, 32, LANES), F32),
            vmem((4, 2, 1, LANES), F32),
            vmem((1, LANES), F32),
            vmem((Z * Y * 2 - 1, 1, LANES), F32),
            vmem((LANES, LANES), F32),
            vmem((8, LANES), F32),
            dma,
            dma,
            dma((3,)),
            pltpu.SemaphoreType.REGULAR((2,)),
            dma,
            dma((4,)),
            dma((2, 2)),
            dma((2, 2)),
            *(dma((2,)) for _ in range(6)),
            dma((4,)),
            dma((2,)),
        ],
        compiler_params=pltpu.CompilerParams(collective_id=0, has_side_effects=True, vmem_limit_bytes=8 << 20),
    )(pltpu.with_memory_space_constraint(local, HBM), pltpu.with_memory_space_constraint(weights, HBM))
    out, chk = pl.pallas_call(
        leave,
        out_shape=(jax.ShapeDtypeStruct((32, rows), BF), jax.ShapeDtypeStruct((8, 32), BF)),
        in_specs=[pl.BlockSpec(memory_space=pl.ANY)] * 2,
        out_specs=(pl.BlockSpec(memory_space=HBM), pl.BlockSpec(memory_space=HBM)),
        scratch_shapes=[dma((2,))],
        compiler_params=pltpu.CompilerParams(vmem_limit_bytes=1 << 20),
    )(out, chk)
    return out.T, chk


def solution(mesh):
    Z, Y, X = 8, 8, mesh.shape["rep"]
    torus = Mesh(mesh.devices.reshape(Z, Y, 2, X), ("z", "y", "c", "x"))
    dp = ("z", "y", "c")
    return jax.shard_map(
        functools.partial(body, (Z, Y, X)),
        mesh=torus,
        in_specs=(P("x", dp, None, None), P("x", dp, None, None)),
        out_specs=(P(None, dp), P(None, dp)),
        check_vma=False,
    )
```

```python
import functools

import jax
import jax.numpy as jnp
from jax import lax
from jax.experimental import pallas as pl
from jax.experimental.pallas import tpu as pltpu
from jax.sharding import Mesh
from jax.sharding import PartitionSpec as P

MESH = pl.DeviceIdType.MESH
BF, F32 = jnp.bfloat16, jnp.float32
LANES = 128
GROUPS = 2
HBM = pltpu.MemorySpace.HBM


def far_first(n):
    return sorted(range(1, n), key=lambda o: -min(o, n - o))


def near(n):
    return [o for o in far_first(n) if min(o, n - o) <= 2]


def kernel(sizes, limit, g_ref, w_ref, out_ref, chk_ref, own, away, par, wown, wpar, sa, sb, ra, rb, ca, cb, rca, rcb,
           sa2, sb2, ra2, rb2, ca2, cb2, rca2, rcb2, grp, gc, nsend, nrm, xt, chk, own_sem, away_sem, w_sem, hop,
           s0_send, s0_recv, s1_send, s1_recv, c1_send, c1_recv, s2_send, s2_recv, c2_send, c2_recv,
           g_sem, n_sem):
    Z, Y, X = sizes
    YH = Y // 2
    groups = min(GROUPS, Z, Y)
    z, y, c, x = (lax.axis_index(a) for a in ("z", "y", "c", "x"))
    yh, p = y // 2, lax.rem(y, 2)
    other = 1 - c

    def remote(src, dst, send, recv, at):
        pltpu.make_async_remote_copy(
            src_ref=src, dst_ref=dst, send_sem=send, recv_sem=recv, device_id=at, device_id_type=MESH
        ).start()

    def signal(sem, at):
        pl.semaphore_signal(sem, inc=1, device_id=at, device_id_type=MESH)

    def drained(ref, sem):
        pltpu.make_async_copy(ref, ref, sem).wait()

    half = pl.ds(pl.multiple_of(c * 64, 64), 64)
    weights = pltpu.make_async_copy(w_ref, wown, w_sem.at[2])
    weights.start()
    mine = pltpu.make_async_copy(g_ref.at[half], own, own_sem)
    mine.start()
    rest = pl.ds(pl.multiple_of(other * 64, 64), 64)
    theirs = pltpu.make_async_copy(g_ref.at[rest], away, away_sem)
    theirs.start()

    barrier = pltpu.get_barrier_semaphore()
    for o in near(Y):
        signal(barrier, {"y": lax.rem(y + o, Y)})
    for o in near(Z):
        signal(barrier, {"z": lax.rem(z + o, Z)})
    for o in far_first(X):
        signal(barrier, {"x": lax.rem(x + o, X)})
    signal(barrier, {"c": other})
    pl.semaphore_wait(barrier, len(near(Y)) + len(near(Z)) + X)

    for o in near(Y):
        signal(hop.at[0], {"y": lax.rem(y + o, Y)})
    for o in near(Z):
        signal(hop.at[1], {"z": lax.rem(z + o, Z)})
    theirs.wait()
    for q in (2, 3, 0, 1):
        remote(away.at[pl.ds(16 * q, 16)], par.at[q], s0_send, s0_recv.at[q], {"c": other})
    remote(w_ref, wpar, w_sem.at[0], w_sem.at[1], {"c": other})

    eye = lax.broadcasted_iota(jnp.int32, (16, 16), 0) == lax.broadcasted_iota(jnp.int32, (16, 16), 1)

    def columns(ref):
        w = ref[...].astype(F32)
        w = w / jnp.sum(w, axis=1, keepdims=True)
        row = lax.broadcasted_iota(jnp.int32, w.shape, 0)
        cols = []
        for q in range(4):
            one = jnp.sum(jnp.where(row == 4 * c + q, w, 0.0), axis=0, keepdims=True)
            col = jnp.sum(jnp.where(eye, jnp.broadcast_to(one, (16, 16)), 0.0), axis=1, keepdims=True)
            cols.append(jnp.broadcast_to(col, (16, LANES)))
        return cols

    mine.wait()

    def place(t, me, n):
        d = lax.rem(t - me + n, n)
        return jnp.where(d >= n // 2, 2 * d - n, n - 1 - 2 * d)

    def offsets(n, g):
        by_place = sorted(range(n), key=lambda d: rank(d, n))
        return by_place[n // groups * g : n // groups * (g + 1)]

    def portion(ref, g):
        size = ref.shape[-2] // groups
        return pl.ds(size * g, size)

    def spread(k, axis, me, n, s, r, g):
        for o in far_first(n):
            to = lax.rem(me + o, n)
            part = portion(s, g)
            remote(s.at[to, part], r.at[o - 1, part], s1_send.at[k, g], s1_recv.at[k, g], {axis: to})

    def tiles(q):
        for t in range(Z * YH):
            zt, yt = t // YH, t % YH
            lanes = slice(t * LANES, (t + 1) * LANES)
            a = own[16 * q : 16 * q + 16, lanes].astype(F32)
            b = par[q, :, lanes].astype(F32)
            yield zt, 2 * yt + q % 2, a, b

    y_place = [pl.multiple_of(16 * place(t, y, Y), 16) for t in range(Y)]
    z_place = [pl.multiple_of(16 * place(t, z, Z), 16) for t in range(Z)]
    for q in (2, 3, 0, 1):
        drained(par.at[q], s0_recv.at[q])
        for zt, yt, a, b in tiles(q):
            if q < 2:
                sa[yt, pl.ds(z_place[zt], 16), :] = (a + b).astype(BF)
            else:
                sb[zt, pl.ds(y_place[yt], 16), :] = (a + b).astype(BF)
        if q == 3:
            pl.semaphore_wait(hop.at[1], len(near(Z)))
            spread(1, "z", z, Z, sb, rb, 0)
    pl.semaphore_wait(hop.at[0], len(near(Y)))
    spread(0, "y", y, Y, sa, ra, 0)
    for g in range(1, groups):
        spread(1, "z", z, Z, sb, rb, g)
        spread(0, "y", y, Y, sa, ra, g)

    weights.wait()
    w_own = columns(wown)
    drained(wpar, w_sem.at[1])
    w_par = columns(wpar)
    for q in (2, 3, 0, 1):
        for zt, yt, a, b in tiles(q):
            check = jnp.sum(a * w_own[q] + b * w_par[q], axis=0, keepdims=True).astype(BF)
            if q < 2:
                ca[yt, zt : zt + 1, :] = check
            else:
                cb[zt, yt : yt + 1, :] = check
    for k, axis, me, n, cs, cr in ((1, "z", z, Z, cb, rcb), (0, "y", y, Y, ca, rca)):
        for o in far_first(n):
            to = lax.rem(me + o, n)
            remote(cs.at[to], cr.at[o - 1], c1_send.at[k], c1_recv.at[k], {axis: to})

    def arrived(k, r, g):
        drained(r.at[:, portion(r, g)], s1_recv.at[k, g])

    def rank(o, n):
        return 2 * o - n if o >= n // 2 else n - 1 - 2 * o

    def slot_of(o, n):
        return X * rank(o, n) + x

    def block(g, held, me, n, s, r, s2):
        for o in offsets(n, g):
            rows = slice(16 * rank(o, n), 16 * rank(o, n) + 16)
            acc = s[held, rows, :].astype(F32)
            for j in range(r.shape[0]):
                acc += r[j, rows, :].astype(F32)
            s2[lax.rem(me + o, n)] = acc.astype(BF)

    def give(axis, me, n, os, src, dst, send, recv):
        for o in os:
            to = lax.rem(me + o, n)
            for i in [*far_first(X), 0]:
                if o or i:
                    remote(src.at[to], dst.at[slot_of(o, n)], send, recv, {axis: to, "x": lax.rem(x + i, X)})

    def give_tiles(k, g, axis, me, n, s2, r2):
        give(axis, me, n, offsets(n, g), s2, r2, s2_send.at[k, g], s2_recv.at[k, g])

    for g in range(groups):
        arrived(1, rb, g)
        block(g, z, y, Y, sb, rb, sb2)
        if g == 0:
            arrived(0, ra, g)
        give_tiles(1, g, "y", y, Y, sb2, rb2)
        if g:
            arrived(0, ra, g)
        block(g, y, z, Z, sa, ra, sa2)
        give_tiles(0, g, "z", z, Z, sa2, ra2)
    rb2[slot_of(0, Y)] = sb2[y]
    ra2[slot_of(0, Z)] = sa2[z]

    for k, held, axis, me, n, cs, cr, c2, cr2 in (
        (1, z, "y", y, Y, cb, rcb, cb2, rcb2),
        (0, y, "z", z, Z, ca, rca, ca2, rca2),
    ):
        drained(cr, c1_recv.at[k])
        check = cs[held].astype(F32)
        for o in range(cr.shape[0]):
            check += cr[o].astype(F32)
        for t in range(n):
            c2[t] = check[t : t + 1]
        give(axis, me, n, [*far_first(n), 0], c2, cr2, c2_send.at[k], c2_recv.at[k])
        cr2[slot_of(0, n)] = c2[me]

    def share(r2, g):
        size = r2.shape[0] // groups
        return pl.ds(size * g, size - (g == groups - 1))

    low = top = None
    for g in range(groups):
        sums = []
        for k, r2, acc in ((1, rb2, low), (0, ra2, top)):
            drained(r2.at[share(r2, g)], s2_recv.at[k, g])
            size = r2.shape[0] // groups
            for i in range(size * g, size * (g + 1)):
                acc = r2[i].astype(F32) if acc is None else acc + r2[i].astype(F32)
            sums.append(acc)
        low, top = sums
    m = 2 * p + c

    nsend[...] = jnp.sum(top * top + low * low, axis=0, keepdims=True)
    order = sorted(
        ((a, b, k) for a in range(Z) for b in range(Y) for k in range(2) if a or b or k),
        key=lambda o: -(min(o[0], Z - o[0]) + min(o[1], Y - o[1])),
    )
    far = len(order) // 2
    for j, (dz, dy, dc) in enumerate(order):
        at = {"z": lax.rem(z + dz, Z), "y": lax.rem(y + dy, Y), "c": lax.rem(c + dc, 2)}
        remote(nsend, nrm.at[j], n_sem.at[0], n_sem.at[1 + (j < far)], at)
    grp[m, 0:16, :] = top
    grp[m, 16:32, :] = low
    twin = 2 * yh + 1 - p
    mates = ({"y": twin, "c": other}, {"y": twin, "c": c}, {"y": y, "c": other})
    for at in mates:
        remote(grp.at[m], grp.at[m], g_sem.at[0], g_sem.at[1], at)
    for k, cr2 in ((0, rca2), (1, rcb2)):
        drained(cr2.at[pl.ds(0, cr2.shape[0] - 1)], c2_recv.at[k])
        gc[m, k] = jnp.sum(cr2[...], axis=0)
    for at in mates:
        remote(gc.at[m], gc.at[m], g_sem.at[2], g_sem.at[3], at)
    drained(grp.at[pl.ds(0, 3)], g_sem.at[1])
    drained(gc.at[pl.ds(0, 3)], g_sem.at[3])
    parts = []
    for i in range(8):
        core, q = i // 4, i % 4
        parts.append(grp[2 * (q % 2) + core, 16 * (q // 2) : 16 * (q // 2) + 16, :])
        chk[i : i + 1, :] = gc[2 * (q % 2) + core, q // 2]
    xt[...] = jnp.concatenate(parts, axis=0).T
    turned = pltpu.roll(chk[...], lax.rem(LANES - 32 * m, LANES), 1)[:, 0:32]
    columns_out = xt[pl.ds(pl.multiple_of(32 * m, 32), 32), :]

    drained(nrm.at[pl.ds(far, len(order) - far)], n_sem.at[1])
    square = nsend[...] + jnp.sum(nrm[far:], axis=0)
    drained(nrm.at[pl.ds(0, far)], n_sem.at[2])
    square += jnp.sum(nrm[:far], axis=0)
    square = jnp.sum(square, axis=1, keepdims=True)
    factor = jnp.minimum(1.0, limit / jnp.sqrt(square + 1e-06))
    out_ref[...] = (columns_out * factor).astype(BF)
    chk_ref[...] = (turned * factor).astype(BF)

    drained(wown, w_sem.at[0])
    drained(par, s0_send)
    for ref, sem in (
        *((r.at[:, portion(r, g)], s1_send.at[k, g]) for k, r in ((0, ra), (1, rb)) for g in range(groups)),
        *((r.at[share(r, g)], s2_send.at[k, g]) for k, r in ((0, ra2), (1, rb2)) for g in range(groups)),
        (rca, c1_send.at[0]), (rcb, c1_send.at[1]),
        (rca2.at[pl.ds(0, X * Z - 1)], c2_send.at[0]), (rcb2.at[pl.ds(0, X * Y - 1)], c2_send.at[1]),
        (grp.at[pl.ds(0, 3)], g_sem.at[0]), (gc.at[pl.ds(0, 3)], g_sem.at[2]), (nrm, n_sem.at[0]),
    ):
        drained(ref, sem)


def leave(out_ref, chk_ref, to_ref, chk_to_ref, sem):
    copies = [
        pltpu.make_async_copy(out_ref, to_ref, sem.at[0]),
        pltpu.make_async_copy(chk_ref, chk_to_ref, sem.at[1]),
    ]
    for copy in copies:
        copy.start()
    for copy in copies:
        copy.wait()


def body(sizes, grads, check_weights):
    Z, Y, X = sizes
    local, weights = grads[0, 0], check_weights[0, 0]
    rows, width = local.shape
    limit = 2.0 * float((rows * Z * (Y // 2) * LANES) ** 0.5)
    dma = pltpu.SemaphoreType.DMA
    vmem = pltpu.VMEM
    out, chk = pl.pallas_call(
        functools.partial(kernel, sizes, limit),
        out_shape=(jax.ShapeDtypeStruct((32, rows), BF), jax.ShapeDtypeStruct((8, 32), BF)),
        in_specs=[pl.BlockSpec(memory_space=HBM)] * 2,
        out_specs=(pl.BlockSpec(memory_space=vmem), pl.BlockSpec(memory_space=vmem)),
        scratch_shapes=[
            vmem((64, width), BF),
            vmem((64, width), BF),
            vmem((4, 16, width), BF),
            vmem((8, 16), jnp.int32),
            vmem((8, 16), jnp.int32),
            *(vmem((n, 16 * k, LANES), BF) for n, k in ((Y, Z), (Z, Y), (Y - 1, Z), (Z - 1, Y))),
            *(vmem((n, 8, LANES), BF) for n in (Y, Z, Y - 1, Z - 1)),
            *(vmem((n, 16, LANES), BF) for n in (Z, Y, X * Z, X * Y)),
            *(vmem((n, 1, LANES), F32) for n in (Z, Y, X * Z, X * Y)),
            vmem((4, 32, LANES), F32),
            vmem((4, 2, 1, LANES), F32),
            vmem((1, LANES), F32),
            vmem((Z * Y * 2 - 1, 1, LANES), F32),
            vmem((LANES, LANES), F32),
            vmem((8, LANES), F32),
            dma,
            dma,
            dma((3,)),
            pltpu.SemaphoreType.REGULAR((2,)),
            dma,
            dma((4,)),
            dma((2, GROUPS)),
            dma((2, GROUPS)),
            dma((2,)),
            dma((2,)),
            dma((2, GROUPS)),
            dma((2, GROUPS)),
            dma((2,)),
            dma((2,)),
            dma((4,)),
            dma((3,)),
        ],
        compiler_params=pltpu.CompilerParams(collective_id=0, has_side_effects=True, vmem_limit_bytes=8 << 20),
    )(pltpu.with_memory_space_constraint(local, HBM), pltpu.with_memory_space_constraint(weights, HBM))
    out, chk = pl.pallas_call(
        leave,
        out_shape=(jax.ShapeDtypeStruct((32, rows), BF), jax.ShapeDtypeStruct((8, 32), BF)),
        in_specs=[pl.BlockSpec(memory_space=pl.ANY)] * 2,
        out_specs=(pl.BlockSpec(memory_space=HBM), pl.BlockSpec(memory_space=HBM)),
        scratch_shapes=[dma((2,))],
        compiler_params=pltpu.CompilerParams(vmem_limit_bytes=1 << 20),
    )(out, chk)
    return out.T, chk


def solution(mesh):
    Z, Y, X = 8, 8, mesh.shape["rep"]
    torus = Mesh(mesh.devices.reshape(Z, Y, 2, X), ("z", "y", "c", "x"))
    dp = ("z", "y", "c")
    return jax.shard_map(
        functools.partial(body, (Z, Y, X)),
        mesh=torus,
        in_specs=(P("x", dp, None, None), P("x", dp, None, None)),
        out_specs=(P(None, dp), P(None, dp)),
        check_vma=False,
    )
```

```python
import functools

import jax
import jax.numpy as jnp
from jax import lax
from jax.experimental import pallas as pl
from jax.experimental.pallas import tpu as pltpu
from jax.sharding import Mesh
from jax.sharding import PartitionSpec as P

MESH = pl.DeviceIdType.MESH
BF, F32 = jnp.bfloat16, jnp.float32
LANES = 128
GROUPS = 2
HBM = pltpu.MemorySpace.HBM


def far_first(n):
    return sorted(range(1, n), key=lambda o: -min(o, n - o))


def near(n):
    return [o for o in far_first(n) if min(o, n - o) <= 2]


def kernel(sizes, limit, g_ref, w_ref, out_ref, chk_ref, own, away, par, wown, wpar, sa, sb, ra, rb, ca, cb, rca, rcb,
           sa2, sb2, ra2, rb2, ca2, cb2, rca2, rcb2, grp, gc, nsend, nrm, xt, chk, own_sem, away_sem, w_sem, hop,
           s0_send, s0_recv, s1_send, s1_recv, c1_send, c1_recv, s2_send, s2_recv, c2_send, c2_recv,
           g_sem, n_sem):
    Z, Y, X = sizes
    YH = Y // 2
    groups = min(GROUPS, Z, Y)
    z, y, c, x = (lax.axis_index(a) for a in ("z", "y", "c", "x"))
    yh, p = y // 2, lax.rem(y, 2)
    other = 1 - c

    def remote(src, dst, send, recv, at):
        pltpu.make_async_remote_copy(
            src_ref=src, dst_ref=dst, send_sem=send, recv_sem=recv, device_id=at, device_id_type=MESH
        ).start()

    def signal(sem, at):
        pl.semaphore_signal(sem, inc=1, device_id=at, device_id_type=MESH)

    def drained(ref, sem):
        pltpu.make_async_copy(ref, ref, sem).wait()

    half = pl.ds(pl.multiple_of(c * 64, 64), 64)
    weights = pltpu.make_async_copy(w_ref, wown, w_sem.at[2])
    weights.start()
    mine = pltpu.make_async_copy(g_ref.at[half], own, own_sem)
    mine.start()
    rest = pl.ds(pl.multiple_of(other * 64, 64), 64)
    theirs = pltpu.make_async_copy(g_ref.at[rest], away, away_sem)
    theirs.start()

    barrier = pltpu.get_barrier_semaphore()
    for o in near(Y):
        signal(barrier, {"y": lax.rem(y + o, Y)})
    for o in near(Z):
        signal(barrier, {"z": lax.rem(z + o, Z)})
    for o in far_first(X):
        signal(barrier, {"x": lax.rem(x + o, X)})
    signal(barrier, {"c": other})
    pl.semaphore_wait(barrier, len(near(Y)) + len(near(Z)) + X)

    for o in near(Y):
        signal(hop.at[0], {"y": lax.rem(y + o, Y)})
    for o in near(Z):
        signal(hop.at[1], {"z": lax.rem(z + o, Z)})
    theirs.wait()
    for q in (2, 3, 0, 1):
        remote(away.at[pl.ds(16 * q, 16)], par.at[q], s0_send, s0_recv.at[q], {"c": other})
    remote(w_ref, wpar, w_sem.at[0], w_sem.at[1], {"c": other})

    eye = lax.broadcasted_iota(jnp.int32, (16, 16), 0) == lax.broadcasted_iota(jnp.int32, (16, 16), 1)

    def columns(ref):
        w = ref[...].astype(F32)
        w = w / jnp.sum(w, axis=1, keepdims=True)
        row = lax.broadcasted_iota(jnp.int32, w.shape, 0)
        cols = []
        for q in range(4):
            one = jnp.sum(jnp.where(row == 4 * c + q, w, 0.0), axis=0, keepdims=True)
            col = jnp.sum(jnp.where(eye, jnp.broadcast_to(one, (16, 16)), 0.0), axis=1, keepdims=True)
            cols.append(jnp.broadcast_to(col, (16, LANES)))
        return cols

    mine.wait()

    def place(t, me, n):
        d = lax.rem(t - me + n, n)
        return jnp.where(d >= n // 2, 2 * d - n, n - 1 - 2 * d)

    def offsets(n, g):
        by_place = sorted(range(n), key=lambda d: rank(d, n))
        return by_place[n // groups * g : n // groups * (g + 1)]

    def portion(ref, g):
        size = ref.shape[-2] // groups
        return pl.ds(size * g, size)

    def spread(k, axis, me, n, s, r, g):
        for o in far_first(n):
            to = lax.rem(me + o, n)
            part = portion(s, g)
            remote(s.at[to, part], r.at[o - 1, part], s1_send.at[k, g], s1_recv.at[k, g], {axis: to})

    def tiles(q):
        for t in range(Z * YH):
            zt, yt = t // YH, t % YH
            lanes = slice(t * LANES, (t + 1) * LANES)
            a = own[16 * q : 16 * q + 16, lanes].astype(F32)
            b = par[q, :, lanes].astype(F32)
            yield zt, 2 * yt + q % 2, a, b

    y_place = [pl.multiple_of(16 * place(t, y, Y), 16) for t in range(Y)]
    z_place = [pl.multiple_of(16 * place(t, z, Z), 16) for t in range(Z)]
    for q in (2, 3, 0, 1):
        drained(par.at[q], s0_recv.at[q])
        for t in range(Z * YH):
            zt, yt = t // YH, 2 * (t % YH) + q % 2
            lanes = slice(t * LANES, (t + 1) * LANES)
            both = own[16 * q : 16 * q + 16, lanes] + par[q, :, lanes]
            if q < 2:
                sa[yt, pl.ds(z_place[zt], 16), :] = both
            else:
                sb[zt, pl.ds(y_place[yt], 16), :] = both
        if q == 3:
            pl.semaphore_wait(hop.at[1], len(near(Z)))
            spread(1, "z", z, Z, sb, rb, 0)
    pl.semaphore_wait(hop.at[0], len(near(Y)))
    spread(0, "y", y, Y, sa, ra, 0)
    for g in range(1, groups):
        spread(1, "z", z, Z, sb, rb, g)
        spread(0, "y", y, Y, sa, ra, g)

    weights.wait()
    w_own = columns(wown)
    drained(wpar, w_sem.at[1])
    w_par = columns(wpar)
    for q in (2, 3, 0, 1):
        for zt, yt, a, b in tiles(q):
            check = jnp.sum(a * w_own[q] + b * w_par[q], axis=0, keepdims=True).astype(BF)
            if q < 2:
                ca[yt, zt : zt + 1, :] = check
            else:
                cb[zt, yt : yt + 1, :] = check
    for k, axis, me, n, cs, cr in ((1, "z", z, Z, cb, rcb), (0, "y", y, Y, ca, rca)):
        for o in far_first(n):
            to = lax.rem(me + o, n)
            remote(cs.at[to], cr.at[o - 1], c1_send.at[k], c1_recv.at[k], {axis: to})

    def arrived(k, r, g):
        drained(r.at[:, portion(r, g)], s1_recv.at[k, g])

    def rank(o, n):
        return 2 * o - n if o >= n // 2 else n - 1 - 2 * o

    def slot_of(o, n):
        return X * rank(o, n) + x

    def block(g, held, me, n, s, r, s2):
        for o in offsets(n, g):
            rows = slice(16 * rank(o, n), 16 * rank(o, n) + 16)
            acc = s[held, rows, :].astype(F32)
            for j in range(r.shape[0]):
                acc += r[j, rows, :].astype(F32)
            s2[lax.rem(me + o, n)] = acc.astype(BF)

    def give(axis, me, n, os, src, dst, send, recv):
        for o in os:
            to = lax.rem(me + o, n)
            for i in [*far_first(X), 0]:
                if o or i:
                    remote(src.at[to], dst.at[slot_of(o, n)], send, recv, {axis: to, "x": lax.rem(x + i, X)})

    def give_tiles(k, g, axis, me, n, s2, r2):
        give(axis, me, n, offsets(n, g), s2, r2, s2_send.at[k, g], s2_recv.at[k, g])

    for g in range(groups):
        arrived(1, rb, g)
        block(g, z, y, Y, sb, rb, sb2)
        if g == 0:
            arrived(0, ra, g)
        give_tiles(1, g, "y", y, Y, sb2, rb2)
        if g:
            arrived(0, ra, g)
        block(g, y, z, Z, sa, ra, sa2)
        give_tiles(0, g, "z", z, Z, sa2, ra2)
    rb2[slot_of(0, Y)] = sb2[y]
    ra2[slot_of(0, Z)] = sa2[z]

    for k, held, axis, me, n, cs, cr, c2, cr2 in (
        (1, z, "y", y, Y, cb, rcb, cb2, rcb2),
        (0, y, "z", z, Z, ca, rca, ca2, rca2),
    ):
        drained(cr, c1_recv.at[k])
        check = cs[held].astype(F32)
        for o in range(cr.shape[0]):
            check += cr[o].astype(F32)
        for t in range(n):
            c2[t] = check[t : t + 1]
        give(axis, me, n, [*far_first(n), 0], c2, cr2, c2_send.at[k], c2_recv.at[k])
        cr2[slot_of(0, n)] = c2[me]

    def share(r2, g):
        size = r2.shape[0] // groups
        return pl.ds(size * g, size - (g == groups - 1))

    low = top = None
    for g in range(groups):
        sums = []
        for k, r2, acc in ((1, rb2, low), (0, ra2, top)):
            drained(r2.at[share(r2, g)], s2_recv.at[k, g])
            size = r2.shape[0] // groups
            for i in range(size * g, size * (g + 1)):
                acc = r2[i].astype(F32) if acc is None else acc + r2[i].astype(F32)
            sums.append(acc)
        low, top = sums
    m = 2 * p + c

    nsend[...] = jnp.sum(top * top + low * low, axis=0, keepdims=True)
    order = sorted(
        ((a, b, k) for a in range(Z) for b in range(Y) for k in range(2) if a or b or k),
        key=lambda o: -(min(o[0], Z - o[0]) + min(o[1], Y - o[1])),
    )
    far = len(order) // 2
    for j, (dz, dy, dc) in enumerate(order):
        at = {"z": lax.rem(z + dz, Z), "y": lax.rem(y + dy, Y), "c": lax.rem(c + dc, 2)}
        remote(nsend, nrm.at[j], n_sem.at[0], n_sem.at[1 + (j < far)], at)
    grp[m, 0:16, :] = top
    grp[m, 16:32, :] = low
    twin = 2 * yh + 1 - p
    mates = ({"y": twin, "c": other}, {"y": twin, "c": c}, {"y": y, "c": other})
    for at in mates:
        remote(grp.at[m], grp.at[m], g_sem.at[0], g_sem.at[1], at)
    for k, cr2 in ((0, rca2), (1, rcb2)):
        drained(cr2.at[pl.ds(0, cr2.shape[0] - 1)], c2_recv.at[k])
        gc[m, k] = jnp.sum(cr2[...], axis=0)
    for at in mates:
        remote(gc.at[m], gc.at[m], g_sem.at[2], g_sem.at[3], at)
    drained(grp.at[pl.ds(0, 3)], g_sem.at[1])
    drained(gc.at[pl.ds(0, 3)], g_sem.at[3])
    parts = []
    for i in range(8):
        core, q = i // 4, i % 4
        parts.append(grp[2 * (q % 2) + core, 16 * (q // 2) : 16 * (q // 2) + 16, :])
        chk[i : i + 1, :] = gc[2 * (q % 2) + core, q // 2]
    xt[...] = jnp.concatenate(parts, axis=0).T
    turned = pltpu.roll(chk[...], lax.rem(LANES - 32 * m, LANES), 1)[:, 0:32]
    columns_out = xt[pl.ds(pl.multiple_of(32 * m, 32), 32), :]

    drained(nrm.at[pl.ds(far, len(order) - far)], n_sem.at[1])
    square = nsend[...] + jnp.sum(nrm[far:], axis=0)
    drained(nrm.at[pl.ds(0, far)], n_sem.at[2])
    square += jnp.sum(nrm[:far], axis=0)
    square = jnp.sum(square, axis=1, keepdims=True)
    factor = jnp.minimum(1.0, limit / jnp.sqrt(square + 1e-06))
    out_ref[...] = (columns_out * factor).astype(BF)
    chk_ref[...] = (turned * factor).astype(BF)

    drained(wown, w_sem.at[0])
    drained(par, s0_send)
    for ref, sem in (
        *((r.at[:, portion(r, g)], s1_send.at[k, g]) for k, r in ((0, ra), (1, rb)) for g in range(groups)),
        *((r.at[share(r, g)], s2_send.at[k, g]) for k, r in ((0, ra2), (1, rb2)) for g in range(groups)),
        (rca, c1_send.at[0]), (rcb, c1_send.at[1]),
        (rca2.at[pl.ds(0, X * Z - 1)], c2_send.at[0]), (rcb2.at[pl.ds(0, X * Y - 1)], c2_send.at[1]),
        (grp.at[pl.ds(0, 3)], g_sem.at[0]), (gc.at[pl.ds(0, 3)], g_sem.at[2]), (nrm, n_sem.at[0]),
    ):
        drained(ref, sem)


def leave(out_ref, chk_ref, to_ref, chk_to_ref, sem):
    copies = [
        pltpu.make_async_copy(out_ref, to_ref, sem.at[0]),
        pltpu.make_async_copy(chk_ref, chk_to_ref, sem.at[1]),
    ]
    for copy in copies:
        copy.start()
    for copy in copies:
        copy.wait()


def body(sizes, grads, check_weights):
    Z, Y, X = sizes
    local, weights = grads[0, 0], check_weights[0, 0]
    rows, width = local.shape
    limit = 2.0 * float((rows * Z * (Y // 2) * LANES) ** 0.5)
    dma = pltpu.SemaphoreType.DMA
    vmem = pltpu.VMEM
    out, chk = pl.pallas_call(
        functools.partial(kernel, sizes, limit),
        out_shape=(jax.ShapeDtypeStruct((32, rows), BF), jax.ShapeDtypeStruct((8, 32), BF)),
        in_specs=[pl.BlockSpec(memory_space=HBM)] * 2,
        out_specs=(pl.BlockSpec(memory_space=vmem), pl.BlockSpec(memory_space=vmem)),
        scratch_shapes=[
            vmem((64, width), BF),
            vmem((64, width), BF),
            vmem((4, 16, width), BF),
            vmem((8, 16), jnp.int32),
            vmem((8, 16), jnp.int32),
            *(vmem((n, 16 * k, LANES), BF) for n, k in ((Y, Z), (Z, Y), (Y - 1, Z), (Z - 1, Y))),
            *(vmem((n, 8, LANES), BF) for n in (Y, Z, Y - 1, Z - 1)),
            *(vmem((n, 16, LANES), BF) for n in (Z, Y, X * Z, X * Y)),
            *(vmem((n, 1, LANES), F32) for n in (Z, Y, X * Z, X * Y)),
            vmem((4, 32, LANES), F32),
            vmem((4, 2, 1, LANES), F32),
            vmem((1, LANES), F32),
            vmem((Z * Y * 2 - 1, 1, LANES), F32),
            vmem((LANES, LANES), F32),
            vmem((8, LANES), F32),
            dma,
            dma,
            dma((3,)),
            pltpu.SemaphoreType.REGULAR((2,)),
            dma,
            dma((4,)),
            dma((2, GROUPS)),
            dma((2, GROUPS)),
            dma((2,)),
            dma((2,)),
            dma((2, GROUPS)),
            dma((2, GROUPS)),
            dma((2,)),
            dma((2,)),
            dma((4,)),
            dma((3,)),
        ],
        compiler_params=pltpu.CompilerParams(collective_id=0, has_side_effects=True, vmem_limit_bytes=8 << 20),
    )(pltpu.with_memory_space_constraint(local, HBM), pltpu.with_memory_space_constraint(weights, HBM))
    out, chk = pl.pallas_call(
        leave,
        out_shape=(jax.ShapeDtypeStruct((32, rows), BF), jax.ShapeDtypeStruct((8, 32), BF)),
        in_specs=[pl.BlockSpec(memory_space=pl.ANY)] * 2,
        out_specs=(pl.BlockSpec(memory_space=HBM), pl.BlockSpec(memory_space=HBM)),
        scratch_shapes=[dma((2,))],
        compiler_params=pltpu.CompilerParams(vmem_limit_bytes=1 << 20),
    )(out, chk)
    return out.T, chk


def solution(mesh):
    Z, Y, X = 8, 8, mesh.shape["rep"]
    torus = Mesh(mesh.devices.reshape(Z, Y, 2, X), ("z", "y", "c", "x"))
    dp = ("z", "y", "c")
    return jax.shard_map(
        functools.partial(body, (Z, Y, X)),
        mesh=torus,
        in_specs=(P("x", dp, None, None), P("x", dp, None, None)),
        out_specs=(P(None, dp), P(None, dp)),
        check_vma=False,
    )
```

```python
import functools

import jax
import jax.numpy as jnp
from jax import lax
from jax.experimental import pallas as pl
from jax.experimental.pallas import tpu as pltpu
from jax.sharding import Mesh
from jax.sharding import PartitionSpec as P

MESH = pl.DeviceIdType.MESH
BF, F32 = jnp.bfloat16, jnp.float32
LANES = 128
GROUPS = 2
HBM = pltpu.MemorySpace.HBM


def far_first(n):
    return sorted(range(1, n), key=lambda o: -min(o, n - o))


def near(n):
    return [o for o in far_first(n) if min(o, n - o) <= 2]


def kernel(sizes, limit, g_ref, w_ref, out_ref, chk_ref, own, away, par, wown, wpar, sa, sb, ra, rb, ca, cb, rca, rcb,
           sa2, sb2, ra2, rb2, ca2, cb2, rca2, rcb2, grp, gc, nsend, nrm, xt, chk, own_sem, away_sem, w_sem, hop,
           s0_send, s0_recv, s1_send, s1_recv, c1_send, c1_recv, s2_send, s2_recv, c2_send, c2_recv,
           g_sem, n_sem):
    Z, Y, X = sizes
    YH = Y // 2
    groups = min(GROUPS, Z, Y)
    z, y, c, x = (lax.axis_index(a) for a in ("z", "y", "c", "x"))
    yh, p = y // 2, lax.rem(y, 2)
    other = 1 - c

    def remote(src, dst, send, recv, at):
        pltpu.make_async_remote_copy(
            src_ref=src, dst_ref=dst, send_sem=send, recv_sem=recv, device_id=at, device_id_type=MESH
        ).start()

    def signal(sem, at):
        pl.semaphore_signal(sem, inc=1, device_id=at, device_id_type=MESH)

    def drained(ref, sem):
        pltpu.make_async_copy(ref, ref, sem).wait()

    rest = pl.ds(pl.multiple_of(other * 64, 64), 64)
    theirs = pltpu.make_async_copy(g_ref.at[rest], away, away_sem)
    theirs.start()
    half = pl.ds(pl.multiple_of(c * 64, 64), 64)
    mine = pltpu.make_async_copy(g_ref.at[half], own, own_sem)
    mine.start()
    weights = pltpu.make_async_copy(w_ref, wown, w_sem.at[2])
    weights.start()

    barrier = pltpu.get_barrier_semaphore()
    for o in near(Y):
        signal(barrier, {"y": lax.rem(y + o, Y)})
    for o in near(Z):
        signal(barrier, {"z": lax.rem(z + o, Z)})
    for o in far_first(X):
        signal(barrier, {"x": lax.rem(x + o, X)})
    signal(barrier, {"c": other})
    pl.semaphore_wait(barrier, len(near(Y)) + len(near(Z)) + X)

    for o in near(Y):
        signal(hop.at[0], {"y": lax.rem(y + o, Y)})
    for o in near(Z):
        signal(hop.at[1], {"z": lax.rem(z + o, Z)})
    theirs.wait()
    for q in (2, 3, 0, 1):
        remote(away.at[pl.ds(16 * q, 16)], par.at[q], s0_send, s0_recv.at[q], {"c": other})
    remote(w_ref, wpar, w_sem.at[0], w_sem.at[1], {"c": other})

    eye = lax.broadcasted_iota(jnp.int32, (16, 16), 0) == lax.broadcasted_iota(jnp.int32, (16, 16), 1)

    def columns(ref):
        w = ref[...].astype(F32)
        w = w / jnp.sum(w, axis=1, keepdims=True)
        row = lax.broadcasted_iota(jnp.int32, w.shape, 0)
        cols = []
        for q in range(4):
            one = jnp.sum(jnp.where(row == 4 * c + q, w, 0.0), axis=0, keepdims=True)
            col = jnp.sum(jnp.where(eye, jnp.broadcast_to(one, (16, 16)), 0.0), axis=1, keepdims=True)
            cols.append(jnp.broadcast_to(col, (16, LANES)))
        return cols

    mine.wait()

    def place(t, me, n):
        d = lax.rem(t - me + n, n)
        return jnp.where(d >= n // 2, 2 * d - n, n - 1 - 2 * d)

    def offsets(n, g):
        by_place = sorted(range(n), key=lambda d: rank(d, n))
        return by_place[n // groups * g : n // groups * (g + 1)]

    def portion(ref, g):
        size = ref.shape[-2] // groups
        return pl.ds(size * g, size)

    def spread(k, axis, me, n, s, r, g):
        for o in far_first(n):
            to = lax.rem(me + o, n)
            part = portion(s, g)
            remote(s.at[to, part], r.at[o - 1, part], s1_send.at[k, g], s1_recv.at[k, g], {axis: to})

    def tiles(q):
        for t in range(Z * YH):
            zt, yt = t // YH, t % YH
            lanes = slice(t * LANES, (t + 1) * LANES)
            a = own[16 * q : 16 * q + 16, lanes].astype(F32)
            b = par[q, :, lanes].astype(F32)
            yield zt, 2 * yt + q % 2, a, b

    y_place = [pl.multiple_of(16 * place(t, y, Y), 16) for t in range(Y)]
    z_place = [pl.multiple_of(16 * place(t, z, Z), 16) for t in range(Z)]
    for q in (2, 3, 0, 1):
        drained(par.at[q], s0_recv.at[q])
        for t in range(Z * YH):
            zt, yt = t // YH, 2 * (t % YH) + q % 2
            lanes = slice(t * LANES, (t + 1) * LANES)
            both = own[16 * q : 16 * q + 16, lanes] + par[q, :, lanes]
            if q < 2:
                sa[yt, pl.ds(z_place[zt], 16), :] = both
            else:
                sb[zt, pl.ds(y_place[yt], 16), :] = both
        if q == 3:
            pl.semaphore_wait(hop.at[1], len(near(Z)))
            spread(1, "z", z, Z, sb, rb, 0)
    pl.semaphore_wait(hop.at[0], len(near(Y)))
    spread(0, "y", y, Y, sa, ra, 0)
    for g in range(1, groups):
        spread(1, "z", z, Z, sb, rb, g)
        spread(0, "y", y, Y, sa, ra, g)

    weights.wait()
    w_own = columns(wown)
    drained(wpar, w_sem.at[1])
    w_par = columns(wpar)
    for q in (2, 3, 0, 1):
        for zt, yt, a, b in tiles(q):
            check = jnp.sum(a * w_own[q] + b * w_par[q], axis=0, keepdims=True).astype(BF)
            if q < 2:
                ca[yt, zt : zt + 1, :] = check
            else:
                cb[zt, yt : yt + 1, :] = check
    for k, axis, me, n, cs, cr in ((1, "z", z, Z, cb, rcb), (0, "y", y, Y, ca, rca)):
        for o in far_first(n):
            to = lax.rem(me + o, n)
            remote(cs.at[to], cr.at[o - 1], c1_send.at[k], c1_recv.at[k], {axis: to})

    def arrived(k, r, g):
        drained(r.at[:, portion(r, g)], s1_recv.at[k, g])

    def rank(o, n):
        return 2 * o - n if o >= n // 2 else n - 1 - 2 * o

    def slot_of(o, n):
        return X * rank(o, n) + x

    def block(g, held, me, n, s, r, s2):
        for o in offsets(n, g):
            rows = slice(16 * rank(o, n), 16 * rank(o, n) + 16)
            acc = s[held, rows, :].astype(F32)
            for j in range(r.shape[0]):
                acc += r[j, rows, :].astype(F32)
            s2[lax.rem(me + o, n)] = acc.astype(BF)

    def give(axis, me, n, os, src, dst, send, recv):
        for o in os:
            to = lax.rem(me + o, n)
            for i in [*far_first(X), 0]:
                if o or i:
                    remote(src.at[to], dst.at[slot_of(o, n)], send, recv, {axis: to, "x": lax.rem(x + i, X)})

    def give_tiles(k, g, axis, me, n, s2, r2):
        give(axis, me, n, offsets(n, g), s2, r2, s2_send.at[k, g], s2_recv.at[k, g])

    for g in range(groups):
        arrived(1, rb, g)
        block(g, z, y, Y, sb, rb, sb2)
        if g == 0:
            arrived(0, ra, g)
        give_tiles(1, g, "y", y, Y, sb2, rb2)
        if g:
            arrived(0, ra, g)
        block(g, y, z, Z, sa, ra, sa2)
        give_tiles(0, g, "z", z, Z, sa2, ra2)
    rb2[slot_of(0, Y)] = sb2[y]
    ra2[slot_of(0, Z)] = sa2[z]

    for k, held, axis, me, n, cs, cr, c2, cr2 in (
        (1, z, "y", y, Y, cb, rcb, cb2, rcb2),
        (0, y, "z", z, Z, ca, rca, ca2, rca2),
    ):
        drained(cr, c1_recv.at[k])
        check = cs[held].astype(F32)
        for o in range(cr.shape[0]):
            check += cr[o].astype(F32)
        for t in range(n):
            c2[t] = check[t : t + 1]
        give(axis, me, n, [*far_first(n), 0], c2, cr2, c2_send.at[k], c2_recv.at[k])
        cr2[slot_of(0, n)] = c2[me]

    def share(r2, g):
        size = r2.shape[0] // groups
        return pl.ds(size * g, size - (g == groups - 1))

    low = top = None
    for g in range(groups):
        sums = []
        for k, r2, acc in ((1, rb2, low), (0, ra2, top)):
            drained(r2.at[share(r2, g)], s2_recv.at[k, g])
            size = r2.shape[0] // groups
            for i in range(size * g, size * (g + 1)):
                acc = r2[i].astype(F32) if acc is None else acc + r2[i].astype(F32)
            sums.append(acc)
        low, top = sums
    m = 2 * p + c

    nsend[...] = jnp.sum(top * top + low * low, axis=0, keepdims=True)
    order = sorted(
        ((a, b, k) for a in range(Z) for b in range(Y) for k in range(2) if a or b or k),
        key=lambda o: -(min(o[0], Z - o[0]) + min(o[1], Y - o[1])),
    )
    far = len(order) // 8
    for j, (dz, dy, dc) in enumerate(order):
        at = {"z": lax.rem(z + dz, Z), "y": lax.rem(y + dy, Y), "c": lax.rem(c + dc, 2)}
        remote(nsend, nrm.at[j], n_sem.at[0], n_sem.at[1 + (j < far)], at)
    grp[m, 0:16, :] = top
    grp[m, 16:32, :] = low
    twin = 2 * yh + 1 - p
    mates = ({"y": twin, "c": other}, {"y": twin, "c": c}, {"y": y, "c": other})
    for at in mates:
        remote(grp.at[m], grp.at[m], g_sem.at[0], g_sem.at[1], at)
    for k, cr2 in ((0, rca2), (1, rcb2)):
        drained(cr2.at[pl.ds(0, cr2.shape[0] - 1)], c2_recv.at[k])
        gc[m, k] = jnp.sum(cr2[...], axis=0)
    for at in mates:
        remote(gc.at[m], gc.at[m], g_sem.at[2], g_sem.at[3], at)
    drained(grp.at[pl.ds(0, 3)], g_sem.at[1])
    drained(gc.at[pl.ds(0, 3)], g_sem.at[3])
    parts = []
    for i in range(8):
        core, q = i // 4, i % 4
        parts.append(grp[2 * (q % 2) + core, 16 * (q // 2) : 16 * (q // 2) + 16, :])
        chk[i : i + 1, :] = gc[2 * (q % 2) + core, q // 2]
    xt[...] = jnp.concatenate(parts, axis=0).T
    turned = pltpu.roll(chk[...], lax.rem(LANES - 32 * m, LANES), 1)[:, 0:32]
    columns_out = xt[pl.ds(pl.multiple_of(32 * m, 32), 32), :]

    drained(nrm.at[pl.ds(far, len(order) - far)], n_sem.at[1])
    square = nsend[...] + jnp.sum(nrm[far:], axis=0)
    drained(nrm.at[pl.ds(0, far)], n_sem.at[2])
    square += jnp.sum(nrm[:far], axis=0)
    square = jnp.sum(square, axis=1, keepdims=True)
    factor = jnp.minimum(1.0, limit / jnp.sqrt(square + 1e-06))
    out_ref[...] = (columns_out * factor).astype(BF)
    chk_ref[...] = (turned * factor).astype(BF)

    drained(wown, w_sem.at[0])
    drained(par, s0_send)
    for ref, sem in (
        *((r.at[:, portion(r, g)], s1_send.at[k, g]) for k, r in ((0, ra), (1, rb)) for g in range(groups)),
        *((r.at[share(r, g)], s2_send.at[k, g]) for k, r in ((0, ra2), (1, rb2)) for g in range(groups)),
        (rca, c1_send.at[0]), (rcb, c1_send.at[1]),
        (rca2.at[pl.ds(0, X * Z - 1)], c2_send.at[0]), (rcb2.at[pl.ds(0, X * Y - 1)], c2_send.at[1]),
        (grp.at[pl.ds(0, 3)], g_sem.at[0]), (gc.at[pl.ds(0, 3)], g_sem.at[2]), (nrm, n_sem.at[0]),
    ):
        drained(ref, sem)


def leave(out_ref, chk_ref, to_ref, chk_to_ref, sem):
    copies = [
        pltpu.make_async_copy(out_ref, to_ref, sem.at[0]),
        pltpu.make_async_copy(chk_ref, chk_to_ref, sem.at[1]),
    ]
    for copy in copies:
        copy.start()
    for copy in copies:
        copy.wait()


def body(sizes, grads, check_weights):
    Z, Y, X = sizes
    local, weights = grads[0, 0], check_weights[0, 0]
    rows, width = local.shape
    limit = 2.0 * float((rows * Z * (Y // 2) * LANES) ** 0.5)
    dma = pltpu.SemaphoreType.DMA
    vmem = pltpu.VMEM
    out, chk = pl.pallas_call(
        functools.partial(kernel, sizes, limit),
        out_shape=(jax.ShapeDtypeStruct((32, rows), BF), jax.ShapeDtypeStruct((8, 32), BF)),
        in_specs=[pl.BlockSpec(memory_space=HBM)] * 2,
        out_specs=(pl.BlockSpec(memory_space=vmem), pl.BlockSpec(memory_space=vmem)),
        scratch_shapes=[
            vmem((64, width), BF),
            vmem((64, width), BF),
            vmem((4, 16, width), BF),
            vmem((8, 16), jnp.int32),
            vmem((8, 16), jnp.int32),
            *(vmem((n, 16 * k, LANES), BF) for n, k in ((Y, Z), (Z, Y), (Y - 1, Z), (Z - 1, Y))),
            *(vmem((n, 8, LANES), BF) for n in (Y, Z, Y - 1, Z - 1)),
            *(vmem((n, 16, LANES), BF) for n in (Z, Y, X * Z, X * Y)),
            *(vmem((n, 1, LANES), F32) for n in (Z, Y, X * Z, X * Y)),
            vmem((4, 32, LANES), F32),
            vmem((4, 2, 1, LANES), F32),
            vmem((1, LANES), F32),
            vmem((Z * Y * 2 - 1, 1, LANES), F32),
            vmem((LANES, LANES), F32),
            vmem((8, LANES), F32),
            dma,
            dma,
            dma((3,)),
            pltpu.SemaphoreType.REGULAR((2,)),
            dma,
            dma((4,)),
            dma((2, GROUPS)),
            dma((2, GROUPS)),
            dma((2,)),
            dma((2,)),
            dma((2, GROUPS)),
            dma((2, GROUPS)),
            dma((2,)),
            dma((2,)),
            dma((4,)),
            dma((3,)),
        ],
        compiler_params=pltpu.CompilerParams(collective_id=0, has_side_effects=True, vmem_limit_bytes=8 << 20),
    )(pltpu.with_memory_space_constraint(local, HBM), pltpu.with_memory_space_constraint(weights, HBM))
    out, chk = pl.pallas_call(
        leave,
        out_shape=(jax.ShapeDtypeStruct((32, rows), BF), jax.ShapeDtypeStruct((8, 32), BF)),
        in_specs=[pl.BlockSpec(memory_space=pl.ANY)] * 2,
        out_specs=(pl.BlockSpec(memory_space=HBM), pl.BlockSpec(memory_space=HBM)),
        scratch_shapes=[dma((2,))],
        compiler_params=pltpu.CompilerParams(vmem_limit_bytes=1 << 20),
    )(out, chk)
    return out.T, chk


def solution(mesh):
    Z, Y, X = 8, 8, mesh.shape["rep"]
    torus = Mesh(mesh.devices.reshape(Z, Y, 2, X), ("z", "y", "c", "x"))
    dp = ("z", "y", "c")
    return jax.shard_map(
        functools.partial(body, (Z, Y, X)),
        mesh=torus,
        in_specs=(P("x", dp, None, None), P("x", dp, None, None)),
        out_specs=(P(None, dp), P(None, dp)),
        check_vma=False,
    )
```
